128 devices in a mesh: index: 8 (over y, core), bulk: 16 (over z, x).
Axes of the slice: x: 4, y: 4, z: 4, core: 2. Of those that a mesh axis runs over, the one named last changes fastest.
Arguments:
- questions: bfloat16 [4096, 768], P(('index', 'bulk')), may hold values from -26 to 26
- passages: bfloat16 [262144, 768], P(('index', 'bulk')), may hold values from -6 to 6
- candidate_ids: int32 [4096, 32], P(('index', 'bulk')), may hold values from 0 to 262143, as said below
- reader_loglik: float32 [4096, 32], P(('index', 'bulk')), may hold values from -400 to 0
Outputs:
- mean_divergence: float32 [], replicated
- question_grads: float32 [4096, 768], P(('index', 'bulk'))
The draws below stay inside these ranges and needn't reach their ends.
Inputs may be any that keep to these rules, and one draw needn't show every extreme that they name: `candidate_ids`: passage id p lies in the range of owner p // 2048. Among the 32 candidates of the 32 questions of one device, at most 16 lie in one owner's range; in every draw some owner has exactly 16 from every device, and every owner has at least one from every device.
All inputs are finite; a program needn't handle non-finite values.
Results may differ from the reference program's by a relative error of at most 0.0024.
Values may be sent and summed in bfloat16 or wider, within the bound.
No kernel may reach another device: no remote copies, remote signals or barrier semaphores. Data moves between devices by JAX's collectives and lax.ppermute only.
A program may use at most 64 MiB of HBM per device.

```python
import math
import jax
import jax.numpy as jnp
from jax import lax

D = 768
P_DEV = 2048
Q_DEV = 32
K = 32
OWNERS = 128
CAP = 16
QUESTIONS = 4096
PASSAGES = 262144


def passage_rows(key, row_ids):
    base_key = jax.random.fold_in(key, 202)

    def one_row(row_id):
        row_key = jax.random.fold_in(base_key, row_id)
        return jnp.clip(jax.random.normal(row_key, (D,), jnp.float32), -6.0, 6.0)
    return jax.vmap(one_row)(row_ids)


def permute_slots(sub_key):
    return jax.random.permutation(sub_key, OWNERS * CAP)


def permute_pairs(sub_key):
    return jax.random.permutation(sub_key, Q_DEV * K)


def route_plan(key):
    base_key = jax.random.fold_in(key, 303)
    key_list = jax.random.split(base_key, 6)
    popular = jax.random.randint(key_list[0], (OWNERS,), 1, 9)
    weight = popular[None, :] + jax.random.randint(key_list[1], (OWNERS, OWNERS), 0, 3)
    hottest = jax.random.randint(key_list[2], (), 0, OWNERS)
    weight = jnp.where(jnp.arange(OWNERS)[None, :] == hottest, 0, weight)
    slot_rank = jnp.arange(CAP)
    order_key = (slot_rank[None, None, :] * weight[:, :, None]).reshape(OWNERS, OWNERS * CAP)
    tie_break = jax.vmap(permute_slots)(jax.random.split(key_list[3], OWNERS))
    ordered = order_key * (OWNERS * CAP) + tie_break
    chosen = jnp.argsort(ordered, axis=1)[:, :Q_DEV * K]
    shuffle = jax.vmap(permute_pairs)(jax.random.split(key_list[4], OWNERS))
    chosen = jnp.take_along_axis(chosen, shuffle, axis=1)
    owner_of = chosen // CAP
    row_of = jax.random.randint(key_list[5], (OWNERS, Q_DEV * K), 0, P_DEV)
    columns = jnp.arange(Q_DEV * K)[None, :]
    low_place = jnp.argmax((owner_of == 0).astype(jnp.int32), axis=1)
    high_place = jnp.argmax((owner_of == OWNERS - 1).astype(jnp.int32), axis=1)
    row_of = jnp.where(columns == low_place[:, None], 0, row_of)
    row_of = jnp.where(columns == high_place[:, None], P_DEV - 1, row_of)
    return (owner_of * P_DEV + row_of).reshape(QUESTIONS, K).astype(jnp.int32)


def draw_candidate_ids(key, part):
    return route_plan(key)


def draw_passages(key, part):
    return passage_rows(key, jnp.arange(PASSAGES, dtype=jnp.int32)).astype(jnp.bfloat16)


def draw_questions(key, part):
    position = jnp.arange(QUESTIONS).astype(jnp.float32) / max(QUESTIONS - 1, 1)
    key_list = jax.random.split(jax.random.fold_in(key, 404), 1)
    row_scale = 1.0 + 2.0 * position
    return (jnp.clip(jax.random.normal(key_list[0], (QUESTIONS, D), jnp.float32), -6.0, 6.0) * row_scale[:, None]).astype(jnp.bfloat16)


def draw_reader_loglik(key, part):
    position = jnp.arange(QUESTIONS).astype(jnp.float32) / max(QUESTIONS - 1, 1)
    key_list = jax.random.split(jax.random.fold_in(key, 505), 1)
    spread = jax.random.uniform(key_list[0], (QUESTIONS, K), jnp.float32, 0.0, 3.0)
    row_scale = 1.0 + 3.0 * position
    return -row_scale[:, None] * spread


def setup_inputs(seed: int = 0) -> dict:
    keys = jax.random.split(jax.random.key(seed), 5)
    questions = draw_questions(jax.random.fold_in(keys[4], 71), 0)
    passages = draw_passages(jax.random.fold_in(keys[4], 71), 0)
    candidate_ids = draw_candidate_ids(jax.random.fold_in(keys[4], 71), 0)
    reader_loglik = draw_reader_loglik(jax.random.fold_in(keys[4], 71), 0)
    return {"questions": questions, "passages": passages, "candidate_ids": candidate_ids, "reader_loglik": reader_loglik}


def log_normalize(logits):
    highest = lax.optimization_barrier(jnp.max(logits, axis=1, keepdims=True))
    shifted = logits - highest
    return shifted - jnp.log(lax.optimization_barrier(jnp.sum(jnp.exp(shifted), axis=1, keepdims=True)))

def reference(questions, passages, candidate_ids, reader_loglik):
    block_rows = math.gcd(QUESTIONS, 512)
    blocks = QUESTIONS // block_rows
    score_scale = 4.0 / math.sqrt(D)

    def one_block(packed):
        query_rows, id_rows, reader_rows = packed
        gathered = jnp.take(passages, id_rows, axis=0).astype(jnp.float32)
        scores = jnp.einsum('qd,qkd->qk', query_rows.astype(jnp.float32), gathered, precision=lax.Precision.HIGHEST) * score_scale
        log_retriever = log_normalize(scores)
        log_reader = log_normalize(reader_rows)
        reader_prob = jnp.exp(log_reader)
        retriever_prob = jnp.exp(log_retriever)
        divergence = lax.optimization_barrier(jnp.sum(reader_prob * (log_reader - log_retriever), axis=1))
        rounded = (retriever_prob - reader_prob).astype(jnp.bfloat16)
        rounded = lax.optimization_barrier(rounded)
        grads = jnp.einsum('qk,qkd->qd', rounded.astype(jnp.float32), gathered, precision=lax.Precision.HIGHEST) * score_scale
        return (divergence, grads)
    divergence, grads = lax.map(one_block, (questions.reshape(blocks, block_rows, D), candidate_ids.reshape(blocks, block_rows, K), reader_loglik.reshape(blocks, block_rows, K)))
    return (jnp.sum(divergence) / QUESTIONS, grads.reshape(QUESTIONS, D))
```

```python
import math

import jax
import jax.numpy as jnp
from jax import lax
from jax.experimental import pallas as pl
from jax.experimental.pallas import tpu as pltpu
from jax.sharding import PartitionSpec as P

AXES = ("index", "bulk")
LANES = 128
CAP = 16
VMEM = pl.BlockSpec(memory_space=pltpu.VMEM)


def exchange(blocks):
    return lax.all_to_all(blocks, AXES, split_axis=0, concat_axis=0, tiled=True)


def log_normalize(logits):
    highest = jnp.max(logits, axis=1, keepdims=True)
    shifted = logits - highest
    return shifted - jnp.log(jnp.sum(jnp.exp(shifted), axis=1, keepdims=True))


def as_lanes(ref):
    return jnp.concatenate([ref[pl.ds(b, 8, stride=4), :] for b in range(4)], axis=1)


def plan_kernel(ids_ref, reader_ref, request_ref, table_ref, reader_scratch):
    reader_scratch[...] = log_normalize(reader_ref[...])
    ids = as_lanes(ids_ref)
    log_reader = as_lanes(reader_scratch)
    owner = ids >> 11
    row = ids & 2047
    question = 4 * lax.broadcasted_iota(jnp.int32, (8, LANES), 0) + (
        lax.broadcasted_iota(jnp.int32, (8, LANES), 1) >> 5
    )
    high = (row >> 3).astype(jnp.float32)
    low = (((row & 7) << 5) | question).astype(jnp.float32)
    part0 = log_reader.astype(jnp.bfloat16).astype(jnp.float32)
    rest = log_reader - part0
    part1 = rest.astype(jnp.bfloat16).astype(jnp.float32)
    part2 = rest - part1
    owners = lax.broadcasted_iota(jnp.int32, (LANES, LANES), 0)
    member = [
        jnp.where(owner[a : a + 1, :] == owners, 1.0, 0.0).astype(jnp.float32) for a in range(8)
    ]
    member_low = [m.astype(jnp.bfloat16) for m in member]
    before = lax.broadcasted_iota(jnp.int32, (LANES, 2 * LANES), 0)
    after = lax.broadcasted_iota(jnp.int32, (LANES, 2 * LANES), 1)
    prefix = jnp.where((before < after) | (after >= LANES), 1.0, 0.0).astype(jnp.bfloat16)
    counts = jnp.dot(
        jnp.concatenate(member_low, axis=0), prefix, preferred_element_type=jnp.float32
    )
    slots = lax.broadcasted_iota(jnp.int32, (CAP, LANES), 0).astype(jnp.float32)
    carry = jnp.zeros((LANES, LANES), jnp.float32)
    left = []
    for a in range(8):
        block = counts[a * LANES : (a + 1) * LANES, :]
        rank = jnp.sum(member[a] * (block[:, :LANES] + carry), axis=0, keepdims=True)
        carry = carry + block[:, LANES:]
        here = jnp.where(slots == rank, 1.0, 0.0)
        values = [high, low, part0, part1, part2]
        pieces = [here * v[a : a + 1, :] for v in values] + [here]
        left.append(jnp.concatenate(pieces, axis=0).astype(jnp.bfloat16))
    table = lax.dot_general(
        jnp.concatenate(left, axis=1),
        jnp.concatenate(member_low, axis=1),
        (((1,), (1,)), ((), ())),
        preferred_element_type=jnp.float32,
    )
    table_ref[...] = table[CAP:, :]
    wanted = table[:CAP, :].astype(jnp.int32) * 8 + (table[CAP : 2 * CAP, :].astype(jnp.int32) >> 5)
    padded = jnp.concatenate([wanted, jnp.zeros((LANES - CAP, LANES), jnp.int32)], axis=0)
    request_ref[...] = padded.T


def slots_kernel(table_ref, info_ref):
    owners = lax.broadcasted_iota(jnp.int32, (LANES, LANES * CAP), 0)
    lanes = lax.broadcasted_iota(jnp.int32, (LANES, LANES * CAP), 1)
    spread = jnp.where((lanes >> 4) == owners, 1.0, 0.0).astype(jnp.bfloat16)
    wide = jnp.dot(
        table_ref[...].astype(jnp.bfloat16), spread, preferred_element_type=jnp.float32
    )
    own = (lanes[:CAP] & (CAP - 1)) == owners[:CAP]

    def pick(n):
        return jnp.sum(
            jnp.where(own, wide[n * CAP : (n + 1) * CAP, :], 0.0), axis=0, keepdims=True
        )

    question = pick(0).astype(jnp.int32) & 31
    question = jnp.where(pick(4) > 0.5, question, -1).astype(jnp.float32)
    log_reader = pick(1) + pick(2) + pick(3)
    info_ref[...] = jnp.concatenate(
        [question, log_reader, jnp.zeros((6, LANES * CAP), jnp.float32)], axis=0
    )


def fetch_kernel(wanted_ref, passages_ref, rows_ref, image, dense, index, sem):
    chunks = image.shape[0]
    total = jnp.zeros((CAP, LANES), jnp.int32)
    for k in range(8):
        part = wanted_ref[pl.ds(k, 16, stride=8), :]
        total = total + (pltpu.roll(part, CAP * k, 1) if k else part)
    dense[...] = total
    copy = pltpu.make_async_copy(dense, index, sem)
    copy.start()
    for c in range(chunks):
        image[c] = passages_ref[:, c * LANES : (c + 1) * LANES].astype(jnp.float32)
    copy.wait()
    sub = lax.broadcasted_iota(jnp.int32, (8, LANES), 0)

    def one_block(d, _):
        high = d >> 3
        low = (d & 7) * CAP
        halves = []
        for h in range(2):
            acc = None
            for j in range(8):
                r = index[high, low + h * 8 + j]
                got = [image[c, pl.ds(r, 8, stride=0), :] for c in range(chunks)]
                acc = got if acc is None else [jnp.where(sub == j, g, x) for g, x in zip(got, acc)]
            halves.append(acc)
        start = pl.multiple_of(d * CAP, CAP)
        for c in range(chunks):
            pair = jnp.concatenate([halves[0][c], halves[1][c]], axis=0).astype(jnp.bfloat16)
            rows_ref[pl.ds(start, CAP), c * LANES : (c + 1) * LANES] = pair
        return 0

    lax.fori_loop(0, LANES, one_block, 0)


def score_kernel(questions_ref, rows_ref, info_ref, grads_ref, part_ref):
    count, width = questions_ref.shape
    scale = 4.0 / math.sqrt(width)
    scores = (
        lax.dot_general(
            questions_ref[...],
            rows_ref[...],
            (((1,), (1,)), ((), ())),
            preferred_element_type=jnp.float32,
        )
        * scale
    )
    question = info_ref[0:1, :]
    log_reader = info_ref[1:2, :]
    mine = question == lax.broadcasted_iota(jnp.int32, scores.shape, 0).astype(jnp.float32)
    highest = jnp.max(jnp.where(mine, scores, -jnp.inf), axis=1, keepdims=True)
    shifted = jnp.where(mine, scores - highest, -jnp.inf)
    log_retriever = shifted - jnp.log(jnp.sum(jnp.exp(shifted), axis=1, keepdims=True))
    reader = jnp.exp(log_reader)
    weights = jnp.where(mine, jnp.exp(log_retriever) - reader, 0.0).astype(jnp.bfloat16)
    grads_ref[...] = (
        jnp.dot(weights, rows_ref[...], preferred_element_type=jnp.float32) * scale
    )
    own = jnp.sum(jnp.where(mine, log_retriever, 0.0), axis=0, keepdims=True)
    divergence = jnp.where(question >= 0.0, reader * (log_reader - own), 0.0)
    part_ref[...] = jnp.broadcast_to(jnp.sum(divergence, axis=1, keepdims=True), part_ref.shape)


def body(questions, passages, candidate_ids, reader_loglik):
    owners = lax.axis_size(AXES)
    question_count, width = questions.shape
    slot_count = owners * CAP
    request, table = pl.pallas_call(
        plan_kernel,
        out_shape=(
            jax.ShapeDtypeStruct((owners, LANES), jnp.int32),
            jax.ShapeDtypeStruct((5 * CAP, LANES), jnp.float32),
        ),
        in_specs=[VMEM, VMEM],
        out_specs=(VMEM, VMEM),
        scratch_shapes=[pltpu.VMEM(reader_loglik.shape, jnp.float32)],
        name="plan",
    )(candidate_ids, reader_loglik)
    wanted = exchange(request)
    info = pl.pallas_call(
        slots_kernel,
        out_shape=jax.ShapeDtypeStruct((8, slot_count), jnp.float32),
        in_specs=[VMEM],
        out_specs=VMEM,
        name="slots",
    )(table)
    fetched = pl.pallas_call(
        fetch_kernel,
        out_shape=jax.ShapeDtypeStruct((slot_count, width), passages.dtype),
        in_specs=[VMEM, VMEM],
        out_specs=VMEM,
        scratch_shapes=[
            pltpu.VMEM((width // LANES, passages.shape[0], LANES), jnp.float32),
            pltpu.VMEM((CAP, LANES), jnp.int32),
            pltpu.SMEM((CAP, LANES), jnp.int32),
            pltpu.SemaphoreType.DMA,
        ],
        name="fetch",
    )(wanted, passages)
    replies = exchange(fetched.reshape(owners, CAP, width)).reshape(slot_count, width)
    grads, part = pl.pallas_call(
        score_kernel,
        out_shape=(
            jax.ShapeDtypeStruct((question_count, width), jnp.float32),
            jax.ShapeDtypeStruct((owners, LANES), jnp.float32),
        ),
        in_specs=[VMEM, VMEM, VMEM],
        out_specs=(VMEM, VMEM),
        name="score",
    )(questions, replies, info)
    summed = jnp.sum(exchange(part), axis=0)[0]
    return (summed / (question_count * owners), grads)


def solution(mesh):
    placed = P(AXES, None)
    return jax.shard_map(
        body,
        mesh=mesh,
        in_specs=(placed, placed, placed, placed),
        out_specs=(P(), placed),
        check_vma=False,
    )
```

```python
import math

import jax
import jax.numpy as jnp
from jax import lax
from jax.experimental import pallas as pl
from jax.experimental.pallas import tpu as pltpu
from jax.sharding import PartitionSpec as P

AXES = ("index", "bulk")
LANES = 128
CAP = 16
VMEM = pl.BlockSpec(memory_space=pltpu.VMEM)
HBM = pl.BlockSpec(memory_space=pltpu.HBM)
PARAMS = pltpu.CompilerParams(vmem_limit_bytes=24 << 20)


def in_vmem(array):
    return pltpu.with_memory_space_constraint(array, pltpu.VMEM)


def exchange(blocks):
    return lax.all_to_all(blocks, AXES, split_axis=0, concat_axis=0, tiled=True)


def log_normalize(logits):
    highest = jnp.max(logits, axis=1, keepdims=True)
    shifted = logits - highest
    return shifted - jnp.log(jnp.sum(jnp.exp(shifted), axis=1, keepdims=True))


def as_lanes(ref):
    return jnp.concatenate([ref[pl.ds(b, 8, stride=4), :] for b in range(4)], axis=1)


def members(owner):
    owners = lax.broadcasted_iota(jnp.int32, (LANES, LANES), 0)
    return [jnp.where(owner[a : a + 1, :] == owners, 1.0, 0.0) for a in range(8)]


def placements(member, values):
    member_low = [m.astype(jnp.bfloat16) for m in member]
    before = lax.broadcasted_iota(jnp.int32, (LANES, 2 * LANES), 0)
    after = lax.broadcasted_iota(jnp.int32, (LANES, 2 * LANES), 1)
    prefix = jnp.where((before < after) | (after >= LANES), 1.0, 0.0).astype(jnp.bfloat16)
    counts = jnp.dot(
        jnp.concatenate(member_low, axis=0), prefix, preferred_element_type=jnp.float32
    )
    slots = lax.broadcasted_iota(jnp.int32, (CAP, LANES), 0).astype(jnp.float32)
    carry = jnp.zeros((LANES, LANES), jnp.float32)
    left = []
    for a in range(8):
        block = counts[a * LANES : (a + 1) * LANES, :]
        rank = jnp.sum(member[a] * (block[:, :LANES] + carry), axis=0, keepdims=True)
        carry = carry + block[:, LANES:]
        here = jnp.where(slots == rank, 1.0, 0.0)
        pieces = [here if v is None else here * v[a : a + 1, :] for v in values]
        left.append(jnp.concatenate(pieces, axis=0).astype(jnp.bfloat16))
    return lax.dot_general(
        jnp.concatenate(left, axis=1),
        jnp.concatenate(member_low, axis=1),
        (((1,), (1,)), ((), ())),
        preferred_element_type=jnp.float32,
    )


def plan_kernel(ids_ref, passages_ref, request_ref, local_ref, sem):
    copy = pltpu.make_async_copy(passages_ref, local_ref, sem)
    copy.start()
    ids = as_lanes(ids_ref)
    row = ids & 2047
    high = (row >> 4).astype(jnp.float32)
    low = (row & 15).astype(jnp.float32)
    table = placements(members(ids >> 11), [high, low])
    wanted = (table[:CAP, :] * 16.0 + table[CAP:, :]).astype(jnp.int32)
    padded = jnp.concatenate([wanted, jnp.zeros((LANES - CAP, LANES), jnp.int32)], axis=0)
    request_ref[...] = padded.T
    copy.wait()


def slots_kernel(ids_ref, reader_ref, info_ref, reader_scratch):
    reader_scratch[...] = log_normalize(reader_ref[...])
    ids = as_lanes(ids_ref)
    log_reader = as_lanes(reader_scratch)
    question = 4 * lax.broadcasted_iota(jnp.int32, (8, LANES), 0) + (
        lax.broadcasted_iota(jnp.int32, (8, LANES), 1) >> 5
    )
    part0 = log_reader.astype(jnp.bfloat16).astype(jnp.float32)
    rest = log_reader - part0
    part1 = rest.astype(jnp.bfloat16).astype(jnp.float32)
    part2 = rest - part1
    table = placements(
        members(ids >> 11), [(question + 1).astype(jnp.float32), part0, part1, part2]
    )
    owners = lax.broadcasted_iota(jnp.int32, (LANES, LANES * CAP), 0)
    lanes = lax.broadcasted_iota(jnp.int32, (LANES, LANES * CAP), 1)
    spread = jnp.where((lanes >> 4) == owners, 1.0, 0.0).astype(jnp.bfloat16)
    wide = jnp.dot(table.astype(jnp.bfloat16), spread, preferred_element_type=jnp.float32)
    own = (lanes[:CAP] & (CAP - 1)) == owners[:CAP]

    def pick(n):
        return jnp.sum(
            jnp.where(own, wide[n * CAP : (n + 1) * CAP, :], 0.0), axis=0, keepdims=True
        )

    info_ref[...] = jnp.concatenate(
        [
            pick(0) - 1.0,
            pick(1) + pick(2) + pick(3),
            jnp.zeros((6, LANES * CAP), jnp.float32),
        ],
        axis=0,
    )


def fetch_kernel(wanted_ref, passages_ref, out_ref, image, rows, dense, index, sem, sends):
    chunks = image.shape[0]
    total = jnp.zeros((CAP, LANES), jnp.int32)
    for k in range(8):
        part = wanted_ref[pl.ds(k, 16, stride=8), :]
        total = total + (pltpu.roll(part, CAP * k, 1) if k else part)
    dense[...] = total
    copy = pltpu.make_async_copy(dense, index, sem)
    copy.start()
    for c in range(chunks):
        image[c, 8 : 8 + passages_ref.shape[0], :] = passages_ref[:, c * LANES : (c + 1) * LANES].astype(jnp.float32)
    copy.wait()
    sub = lax.broadcasted_iota(jnp.int32, (8, LANES), 0)

    def send(line):
        part = pl.ds(pl.multiple_of(line * LANES, LANES), LANES)
        return pltpu.make_async_copy(rows.at[part, :], out_ref.at[part, :], sends.at[line])

    def one_line(line, _):
        for d in range(8):
            halves = []
            for h in range(2):
                acc = None
                for j in range(8):
                    r = index[line, d * CAP + h * 8 + j]
                    got = [image[c, pl.ds(r + (8 - j), 8), :] for c in range(chunks)]
                    acc = (
                        got if acc is None else [jnp.where(sub == j, g, x) for g, x in zip(got, acc)]
                    )
                halves.append(acc)
            start = pl.multiple_of(line * LANES + d * CAP, CAP)
            for c in range(chunks):
                pair = jnp.concatenate([halves[0][c], halves[1][c]], axis=0).astype(jnp.bfloat16)
                rows[pl.ds(start, CAP), c * LANES : (c + 1) * LANES] = pair
        send(line).start()
        return 0

    lax.fori_loop(0, CAP, one_line, 0)
    for line in range(CAP):
        send(line).wait()


def score_kernel(questions_ref, rows_ref, info_ref, grads_ref, part_ref):
    count, width = questions_ref.shape
    scale = 4.0 / math.sqrt(width)
    scores = (
        lax.dot_general(
            questions_ref[...],
            rows_ref[...],
            (((1,), (1,)), ((), ())),
            preferred_element_type=jnp.float32,
        )
        * scale
    )
    question = info_ref[0:1, :]
    log_reader = info_ref[1:2, :]
    mine = question == lax.broadcasted_iota(jnp.int32, scores.shape, 0).astype(jnp.float32)
    highest = jnp.max(jnp.where(mine, scores, -jnp.inf), axis=1, keepdims=True)
    shifted = jnp.where(mine, scores - highest, -jnp.inf)
    log_retriever = shifted - jnp.log(jnp.sum(jnp.exp(shifted), axis=1, keepdims=True))
    reader = jnp.exp(log_reader)
    weights = jnp.where(mine, jnp.exp(log_retriever) - reader, 0.0).astype(jnp.bfloat16)
    grads_ref[...] = (
        jnp.dot(weights, rows_ref[...], preferred_element_type=jnp.float32) * scale
    )
    own = jnp.sum(jnp.where(mine, log_retriever, 0.0), axis=0, keepdims=True)
    divergence = jnp.where(question >= 0.0, reader * (log_reader - own), 0.0)
    total = jnp.sum(divergence, axis=1, keepdims=True) / (count * part_ref.shape[0])
    part_ref[...] = jnp.broadcast_to(total, part_ref.shape)


def body(questions, passages, candidate_ids, reader_loglik):
    owners = lax.axis_size(AXES)
    question_count, width = questions.shape
    slot_count = owners * CAP
    request, local = pl.pallas_call(
        plan_kernel,
        out_shape=(
            jax.ShapeDtypeStruct((owners, LANES), jnp.int32),
            pltpu.VMEM(passages.shape, passages.dtype),
        ),
        in_specs=[VMEM, HBM],
        out_specs=(VMEM, VMEM),
        scratch_shapes=[pltpu.SemaphoreType.DMA],
        compiler_params=PARAMS,
        name="plan",
    )(candidate_ids, pltpu.with_memory_space_constraint(passages, pltpu.HBM))
    wanted = exchange(request)
    info = pl.pallas_call(
        slots_kernel,
        out_shape=jax.ShapeDtypeStruct((8, slot_count), jnp.float32),
        in_specs=[VMEM, VMEM],
        out_specs=VMEM,
        scratch_shapes=[pltpu.VMEM(reader_loglik.shape, jnp.float32)],
        compiler_params=PARAMS,
        name="slots",
    )(candidate_ids, reader_loglik)
    fetched = pl.pallas_call(
        fetch_kernel,
        out_shape=pltpu.HBM((slot_count, width), passages.dtype),
        in_specs=[VMEM, VMEM],
        out_specs=HBM,
        scratch_shapes=[
            pltpu.VMEM((width // LANES, passages.shape[0] + CAP, LANES), jnp.float32),
            pltpu.VMEM((slot_count, width), passages.dtype),
            pltpu.VMEM((CAP, LANES), jnp.int32),
            pltpu.SMEM((CAP, LANES), jnp.int32),
            pltpu.SemaphoreType.DMA,
            pltpu.SemaphoreType.DMA((CAP,)),
        ],
        compiler_params=PARAMS,
        name="fetch",
    )(wanted, in_vmem(local))
    replies = exchange(fetched.reshape(owners, CAP, width)).reshape(slot_count, width)
    grads, part = pl.pallas_call(
        score_kernel,
        out_shape=(
            jax.ShapeDtypeStruct((question_count, width), jnp.float32),
            jax.ShapeDtypeStruct((owners, LANES), jnp.float32),
        ),
        in_specs=[VMEM, VMEM, VMEM],
        out_specs=(VMEM, VMEM),
        compiler_params=PARAMS,
        name="score",
    )(questions, in_vmem(replies), info)
    return (jnp.sum(exchange(part), axis=0)[0], grads)


def solution(mesh):
    placed = P(AXES, None)
    return jax.shard_map(
        body,
        mesh=mesh,
        in_specs=(placed, placed, placed, placed),
        out_specs=(P(), placed),
        check_vma=False,
    )
```

```python
import math

import jax
import jax.numpy as jnp
from jax import lax
from jax.experimental import pallas as pl
from jax.experimental.pallas import tpu as pltpu
from jax.sharding import PartitionSpec as P

AXES = ("index", "bulk")
LANES = 128
CAP = 16
VMEM = pl.BlockSpec(memory_space=pltpu.VMEM)
HBM = pl.BlockSpec(memory_space=pltpu.HBM)
PARAMS = pltpu.CompilerParams(vmem_limit_bytes=24 << 20)


def in_vmem(array):
    return pltpu.with_memory_space_constraint(array, pltpu.VMEM)


def exchange(blocks):
    return lax.all_to_all(blocks, AXES, split_axis=0, concat_axis=0, tiled=True)


def log_normalize(logits):
    highest = jnp.max(logits, axis=1, keepdims=True)
    shifted = logits - highest
    return shifted - jnp.log(jnp.sum(jnp.exp(shifted), axis=1, keepdims=True))


def as_lanes(ref):
    return jnp.concatenate([ref[pl.ds(b, 8, stride=4), :] for b in range(4)], axis=1)


def members(owner):
    owners = lax.broadcasted_iota(jnp.int32, (LANES, LANES), 0)
    return [jnp.where(owner[a : a + 1, :] == owners, 1.0, 0.0) for a in range(8)]


def placements(member, values):
    member_low = [m.astype(jnp.bfloat16) for m in member]
    before = lax.broadcasted_iota(jnp.int32, (LANES, 2 * LANES), 0)
    after = lax.broadcasted_iota(jnp.int32, (LANES, 2 * LANES), 1)
    prefix = jnp.where((before < after) | (after >= LANES), 1.0, 0.0).astype(jnp.bfloat16)
    counts = jnp.dot(
        jnp.concatenate(member_low, axis=0), prefix, preferred_element_type=jnp.float32
    )
    slots = lax.broadcasted_iota(jnp.int32, (CAP, LANES), 0).astype(jnp.float32)
    carry = jnp.zeros((LANES, LANES), jnp.float32)
    left = []
    for a in range(8):
        block = counts[a * LANES : (a + 1) * LANES, :]
        rank = jnp.sum(member[a] * (block[:, :LANES] + carry), axis=0, keepdims=True)
        carry = carry + block[:, LANES:]
        here = jnp.where(slots == rank, 1.0, 0.0)
        pieces = [here if v is None else here * v[a : a + 1, :] for v in values]
        left.append(jnp.concatenate(pieces, axis=0).astype(jnp.bfloat16))
    return lax.dot_general(
        jnp.concatenate(left, axis=1),
        jnp.concatenate(member_low, axis=1),
        (((1,), (1,)), ((), ())),
        preferred_element_type=jnp.float32,
    )


def plan_kernel(ids_ref, request_ref):
    ids = as_lanes(ids_ref)
    row = ids & 2047
    high = (row >> 4).astype(jnp.float32)
    low = (row & 15).astype(jnp.float32)
    table = placements(members(ids >> 11), [high, low])
    wanted = (table[:CAP, :] * 16.0 + table[CAP:, :]).astype(jnp.int32)
    padded = jnp.concatenate([wanted, jnp.zeros((LANES - CAP, LANES), jnp.int32)], axis=0)
    request_ref[...] = padded.T


def load_kernel(passages_ref, local_ref, sem):
    copy = pltpu.make_async_copy(passages_ref, local_ref, sem)
    copy.start()
    copy.wait()


def slots_kernel(ids_ref, reader_ref, info_ref, reader_scratch):
    reader_scratch[...] = log_normalize(reader_ref[...])
    ids = as_lanes(ids_ref)
    log_reader = as_lanes(reader_scratch)
    question = 4 * lax.broadcasted_iota(jnp.int32, (8, LANES), 0) + (
        lax.broadcasted_iota(jnp.int32, (8, LANES), 1) >> 5
    )
    part0 = log_reader.astype(jnp.bfloat16).astype(jnp.float32)
    rest = log_reader - part0
    part1 = rest.astype(jnp.bfloat16).astype(jnp.float32)
    part2 = rest - part1
    table = placements(
        members(ids >> 11), [(question + 1).astype(jnp.float32), part0, part1, part2]
    )
    owners = lax.broadcasted_iota(jnp.int32, (LANES, LANES * CAP), 0)
    lanes = lax.broadcasted_iota(jnp.int32, (LANES, LANES * CAP), 1)
    spread = jnp.where((lanes >> 4) == owners, 1.0, 0.0).astype(jnp.bfloat16)
    wide = jnp.dot(table.astype(jnp.bfloat16), spread, preferred_element_type=jnp.float32)
    own = (lanes[:CAP] & (CAP - 1)) == owners[:CAP]

    def pick(n):
        return jnp.sum(
            jnp.where(own, wide[n * CAP : (n + 1) * CAP, :], 0.0), axis=0, keepdims=True
        )

    info_ref[...] = jnp.concatenate(
        [
            pick(0) - 1.0,
            pick(1) + pick(2) + pick(3),
            jnp.zeros((6, LANES * CAP), jnp.float32),
        ],
        axis=0,
    )


def fetch_kernel(wanted_ref, passages_ref, out_ref, image, rows, dense, index, sem, sends):
    chunks = image.shape[0]
    total = jnp.zeros((CAP, LANES), jnp.int32)
    for k in range(8):
        part = wanted_ref[pl.ds(k, 16, stride=8), :]
        total = total + (pltpu.roll(part, CAP * k, 1) if k else part)
    dense[...] = total
    copy = pltpu.make_async_copy(dense, index, sem)
    copy.start()
    for c in range(chunks):
        image[c, 8 : 8 + passages_ref.shape[0], :] = passages_ref[
            :, c * LANES : (c + 1) * LANES
        ].astype(jnp.float32)
    copy.wait()
    sub = lax.broadcasted_iota(jnp.int32, (8, LANES), 0)

    def send(line):
        part = pl.ds(pl.multiple_of(line * LANES, LANES), LANES)
        return pltpu.make_async_copy(rows.at[part, :], out_ref.at[part, :], sends.at[line])

    def one_line(line, _):
        for d in range(8):
            halves = []
            for h in range(2):
                acc = None
                for j in range(8):
                    r = index[line, d * CAP + h * 8 + j]
                    got = [image[c, pl.ds(r + (8 - j), 8), :] for c in range(chunks)]
                    acc = (
                        got if acc is None else [jnp.where(sub == j, g, x) for g, x in zip(got, acc)]
                    )
                halves.append(acc)
            start = pl.multiple_of(line * LANES + d * CAP, CAP)
            for c in range(chunks):
                pair = jnp.concatenate([halves[0][c], halves[1][c]], axis=0).astype(jnp.bfloat16)
                rows[pl.ds(start, CAP), c * LANES : (c + 1) * LANES] = pair
        send(line).start()
        return 0

    lax.fori_loop(0, CAP, one_line, 0)
    for line in range(CAP):
        send(line).wait()


def score_kernel(questions_ref, rows_ref, info_ref, weights_ref, part_ref):
    count, width = questions_ref.shape
    scale = 4.0 / math.sqrt(width)
    scores = (
        lax.dot_general(
            questions_ref[...],
            rows_ref[...],
            (((1,), (1,)), ((), ())),
            preferred_element_type=jnp.float32,
        )
        * scale
    )
    question = info_ref[0:1, :]
    log_reader = info_ref[1:2, :]
    mine = question == lax.broadcasted_iota(jnp.int32, scores.shape, 0).astype(jnp.float32)
    highest = jnp.max(jnp.where(mine, scores, -jnp.inf), axis=1, keepdims=True)
    shifted = jnp.where(mine, scores - highest, -jnp.inf)
    log_retriever = shifted - jnp.log(jnp.sum(jnp.exp(shifted), axis=1, keepdims=True))
    reader = jnp.exp(log_reader)
    weights_ref[...] = jnp.where(mine, jnp.exp(log_retriever) - reader, 0.0).astype(jnp.bfloat16)
    own = jnp.sum(jnp.where(mine, log_retriever, 0.0), axis=0, keepdims=True)
    divergence = jnp.where(question >= 0.0, reader * (log_reader - own), 0.0)
    total = jnp.sum(divergence, axis=1, keepdims=True) / (count * part_ref.shape[0])
    part_ref[...] = jnp.broadcast_to(total, part_ref.shape)


def grads_kernel(weights_ref, rows_ref, grads_ref):
    scale = 4.0 / math.sqrt(rows_ref.shape[1])
    grads_ref[...] = (
        jnp.dot(weights_ref[...], rows_ref[...], preferred_element_type=jnp.float32) * scale
    )


def body(questions, passages, candidate_ids, reader_loglik):
    owners = lax.axis_size(AXES)
    question_count, width = questions.shape
    slot_count = owners * CAP
    request = pl.pallas_call(
        plan_kernel,
        out_shape=pltpu.VMEM((owners, LANES), jnp.int32),
        in_specs=[VMEM],
        out_specs=VMEM,
        compiler_params=PARAMS,
        name="plan",
    )(candidate_ids)
    wanted = exchange(request)
    local = pl.pallas_call(
        load_kernel,
        out_shape=pltpu.VMEM(passages.shape, passages.dtype),
        in_specs=[HBM],
        out_specs=VMEM,
        scratch_shapes=[pltpu.SemaphoreType.DMA],
        compiler_params=PARAMS,
        name="load",
    )(pltpu.with_memory_space_constraint(passages, pltpu.HBM))
    info = pl.pallas_call(
        slots_kernel,
        out_shape=pltpu.VMEM((8, slot_count), jnp.float32),
        in_specs=[VMEM, VMEM],
        out_specs=VMEM,
        scratch_shapes=[pltpu.VMEM(reader_loglik.shape, jnp.float32)],
        compiler_params=PARAMS,
        name="slots",
    )(candidate_ids, reader_loglik)
    fetched = pl.pallas_call(
        fetch_kernel,
        out_shape=pltpu.HBM((slot_count, width), passages.dtype),
        in_specs=[VMEM, VMEM],
        out_specs=HBM,
        scratch_shapes=[
            pltpu.VMEM((width // LANES, passages.shape[0] + CAP, LANES), jnp.float32),
            pltpu.VMEM((slot_count, width), passages.dtype),
            pltpu.VMEM((CAP, LANES), jnp.int32),
            pltpu.SMEM((CAP, LANES), jnp.int32),
            pltpu.SemaphoreType.DMA,
            pltpu.SemaphoreType.DMA((CAP,)),
        ],
        compiler_params=PARAMS,
        name="fetch",
    )(wanted, in_vmem(local))
    replies = exchange(fetched.reshape(owners, CAP, width)).reshape(slot_count, width)
    replies = in_vmem(replies)
    weights, part = pl.pallas_call(
        score_kernel,
        out_shape=(
            pltpu.VMEM((question_count, slot_count), jnp.bfloat16),
            pltpu.VMEM((owners, LANES), jnp.float32),
        ),
        in_specs=[VMEM, VMEM, VMEM],
        out_specs=(VMEM, VMEM),
        compiler_params=PARAMS,
        name="score",
    )(questions, replies, info)
    summed = exchange(part)
    grads = pl.pallas_call(
        grads_kernel,
        out_shape=jax.ShapeDtypeStruct((question_count, width), jnp.float32),
        in_specs=[VMEM, VMEM],
        out_specs=VMEM,
        compiler_params=PARAMS,
        name="grads",
    )(weights, replies)
    return (jnp.sum(summed, axis=0)[0], grads)


def solution(mesh):
    placed = P(AXES, None)
    return jax.shard_map(
        body,
        mesh=mesh,
        in_specs=(placed, placed, placed, placed),
        out_specs=(P(), placed),
        check_vma=False,
    )
```

```python
import math

import jax
import jax.numpy as jnp
from jax import lax
from jax.experimental import pallas as pl
from jax.experimental.pallas import tpu as pltpu
from jax.sharding import PartitionSpec as P

AXES = ("index", "bulk")
LANES = 128
CAP = 16
VMEM = pl.BlockSpec(memory_space=pltpu.VMEM)
HBM = pl.BlockSpec(memory_space=pltpu.HBM)
PARAMS = pltpu.CompilerParams(vmem_limit_bytes=24 << 20)


def in_vmem(array):
    return pltpu.with_memory_space_constraint(array, pltpu.VMEM)


def in_hbm(array):
    return pltpu.with_memory_space_constraint(array, pltpu.HBM)


def exchange(blocks):
    return lax.all_to_all(blocks, AXES, split_axis=0, concat_axis=0, tiled=True)


def log_normalize(logits):
    highest = jnp.max(logits, axis=1, keepdims=True)
    shifted = logits - highest
    return shifted - jnp.log(jnp.sum(jnp.exp(shifted), axis=1, keepdims=True))


def as_lanes(ref):
    return jnp.concatenate([ref[pl.ds(b, 8, stride=4), :] for b in range(4)], axis=1)


def members(owner):
    owners = lax.broadcasted_iota(jnp.int32, (LANES, LANES), 0)
    return [jnp.where(owner[a : a + 1, :] == owners, 1.0, 0.0) for a in range(8)]


def placements(member, values):
    member_low = [m.astype(jnp.bfloat16) for m in member]
    before = lax.broadcasted_iota(jnp.int32, (LANES, 2 * LANES), 0)
    after = lax.broadcasted_iota(jnp.int32, (LANES, 2 * LANES), 1)
    prefix = jnp.where((before < after) | (after >= LANES), 1.0, 0.0).astype(jnp.bfloat16)
    counts = jnp.dot(
        jnp.concatenate(member_low, axis=0), prefix, preferred_element_type=jnp.float32
    )
    slots = lax.broadcasted_iota(jnp.int32, (CAP, LANES), 0).astype(jnp.float32)
    carry = jnp.zeros((LANES, LANES), jnp.float32)
    left = []
    for a in range(8):
        block = counts[a * LANES : (a + 1) * LANES, :]
        rank = jnp.sum(member[a] * (block[:, :LANES] + carry), axis=0, keepdims=True)
        carry = carry + block[:, LANES:]
        here = jnp.where(slots == rank, 1.0, 0.0)
        pieces = [here if v is None else here * v[a : a + 1, :] for v in values]
        left.append(jnp.concatenate(pieces, axis=0).astype(jnp.bfloat16))
    return lax.dot_general(
        jnp.concatenate(left, axis=1),
        jnp.concatenate(member_low, axis=1),
        (((1,), (1,)), ((), ())),
        preferred_element_type=jnp.float32,
    )


def plan_kernel(ids_ref, request_ref):
    ids = as_lanes(ids_ref)
    row = ids & 2047
    high = (row >> 4).astype(jnp.float32)
    low = (row & 15).astype(jnp.float32)
    table = placements(members(ids >> 11), [high, low])
    wanted = (table[:CAP, :] * 16.0 + table[CAP:, :]).astype(jnp.int32)
    padded = jnp.concatenate([wanted, jnp.zeros((LANES - CAP, LANES), jnp.int32)], axis=0)
    request_ref[...] = padded.T


def prepare_kernel(
    ids_hbm, reader_hbm, passages_ref, info_ref, local_ref, ids_ref, reader_scratch, sems
):
    pairs = ((reader_hbm, reader_scratch), (ids_hbm, ids_ref), (passages_ref, local_ref))
    copies = [pltpu.make_async_copy(a, b, sems.at[n]) for n, (a, b) in enumerate(pairs)]
    for copy in copies:
        copy.start()
    copies[0].wait()
    reader_scratch[...] = log_normalize(reader_scratch[...])
    copies[1].wait()
    ids = as_lanes(ids_ref)
    log_reader = as_lanes(reader_scratch)
    question = 4 * lax.broadcasted_iota(jnp.int32, (8, LANES), 0) + (
        lax.broadcasted_iota(jnp.int32, (8, LANES), 1) >> 5
    )
    part0 = log_reader.astype(jnp.bfloat16).astype(jnp.float32)
    rest = log_reader - part0
    part1 = rest.astype(jnp.bfloat16).astype(jnp.float32)
    part2 = rest - part1
    table = placements(
        members(ids >> 11), [(question + 1).astype(jnp.float32), part0, part1, part2]
    )
    owners = lax.broadcasted_iota(jnp.int32, (LANES, LANES * CAP), 0)
    lanes = lax.broadcasted_iota(jnp.int32, (LANES, LANES * CAP), 1)
    spread = jnp.where((lanes >> 4) == owners, 1.0, 0.0).astype(jnp.bfloat16)
    wide = jnp.dot(table.astype(jnp.bfloat16), spread, preferred_element_type=jnp.float32)
    own = (lanes[:CAP] & (CAP - 1)) == owners[:CAP]

    def pick(n):
        return jnp.sum(
            jnp.where(own, wide[n * CAP : (n + 1) * CAP, :], 0.0), axis=0, keepdims=True
        )

    info_ref[...] = jnp.concatenate(
        [
            pick(0) - 1.0,
            pick(1) + pick(2) + pick(3),
            jnp.zeros((6, LANES * CAP), jnp.float32),
        ],
        axis=0,
    )
    copies[2].wait()


def fetch_kernel(wanted_ref, passages_ref, rows, image, dense, index, sem):
    chunks = image.shape[0]
    total = jnp.zeros((CAP, LANES), jnp.int32)
    for k in range(8):
        part = wanted_ref[pl.ds(k, 16, stride=8), :]
        total = total + (pltpu.roll(part, CAP * k, 1) if k else part)
    dense[...] = total
    copy = pltpu.make_async_copy(dense, index, sem)
    copy.start()
    for c in range(chunks):
        image[c, 8 : 8 + passages_ref.shape[0], :] = passages_ref[
            :, c * LANES : (c + 1) * LANES
        ].astype(jnp.float32)
    copy.wait()
    sub = lax.broadcasted_iota(jnp.int32, (8, LANES), 0)

    def one_line(line, _):
        for d in range(8):
            halves = []
            for h in range(2):
                acc = None
                for j in range(8):
                    r = index[line, d * CAP + h * 8 + j]
                    got = [image[c, pl.ds(r + (8 - j), 8), :] for c in range(chunks)]
                    acc = (
                        got if acc is None else [jnp.where(sub == j, g, x) for g, x in zip(got, acc)]
                    )
                halves.append(acc)
            start = pl.multiple_of(line * LANES + d * CAP, CAP)
            for c in range(chunks):
                pair = jnp.concatenate([halves[0][c], halves[1][c]], axis=0).astype(jnp.bfloat16)
                rows[pl.ds(start, CAP), c * LANES : (c + 1) * LANES] = pair
        return 0

    lax.fori_loop(0, CAP, one_line, 0)


def score_kernel(questions_ref, rows_ref, info_ref, weights_ref, part_ref):
    count, width = questions_ref.shape
    scale = 4.0 / math.sqrt(width)
    scores = (
        lax.dot_general(
            questions_ref[...],
            rows_ref[...],
            (((1,), (1,)), ((), ())),
            preferred_element_type=jnp.float32,
        )
        * scale
    )
    question = info_ref[0:1, :]
    log_reader = info_ref[1:2, :]
    mine = question == lax.broadcasted_iota(jnp.int32, scores.shape, 0).astype(jnp.float32)
    highest = jnp.max(jnp.where(mine, scores, -jnp.inf), axis=1, keepdims=True)
    shifted = jnp.where(mine, scores - highest, -jnp.inf)
    log_retriever = shifted - jnp.log(jnp.sum(jnp.exp(shifted), axis=1, keepdims=True))
    reader = jnp.exp(log_reader)
    weights_ref[...] = jnp.where(mine, jnp.exp(log_retriever) - reader, 0.0).astype(jnp.bfloat16)
    own = jnp.sum(jnp.where(mine, log_retriever, 0.0), axis=0, keepdims=True)
    divergence = jnp.where(question >= 0.0, reader * (log_reader - own), 0.0)
    total = jnp.sum(divergence, axis=1, keepdims=True) / (count * part_ref.shape[0])
    part_ref[...] = jnp.broadcast_to(total, part_ref.shape)


def grads_kernel(weights_ref, rows_ref, grads_ref):
    scale = 4.0 / math.sqrt(rows_ref.shape[1])
    grads_ref[...] = (
        jnp.dot(weights_ref[...], rows_ref[...], preferred_element_type=jnp.float32) * scale
    )


def body(questions, passages, candidate_ids, reader_loglik):
    owners = lax.axis_size(AXES)
    question_count, width = questions.shape
    slot_count = owners * CAP
    request = pl.pallas_call(
        plan_kernel,
        out_shape=pltpu.VMEM((owners, LANES), jnp.int32),
        in_specs=[VMEM],
        out_specs=VMEM,
        compiler_params=PARAMS,
        name="plan",
    )(candidate_ids)
    wanted = exchange(request)
    info, local = pl.pallas_call(
        prepare_kernel,
        out_shape=(
            pltpu.VMEM((8, slot_count), jnp.float32),
            pltpu.VMEM(passages.shape, passages.dtype),
        ),
        in_specs=[HBM, HBM, HBM],
        out_specs=(VMEM, VMEM),
        scratch_shapes=[
            pltpu.VMEM(candidate_ids.shape, jnp.int32),
            pltpu.VMEM(reader_loglik.shape, jnp.float32),
            pltpu.SemaphoreType.DMA((3,)),
        ],
        compiler_params=PARAMS,
        name="prepare",
    )(in_hbm(candidate_ids), in_hbm(reader_loglik), in_hbm(passages))
    fetched = pl.pallas_call(
        fetch_kernel,
        out_shape=pltpu.VMEM((slot_count, width), passages.dtype),
        in_specs=[VMEM, VMEM],
        out_specs=VMEM,
        scratch_shapes=[
            pltpu.VMEM((width // LANES, passages.shape[0] + CAP, LANES), jnp.float32),
            pltpu.VMEM((CAP, LANES), jnp.int32),
            pltpu.SMEM((CAP, LANES), jnp.int32),
            pltpu.SemaphoreType.DMA,
        ],
        compiler_params=PARAMS,
        name="fetch",
    )(wanted, in_vmem(local))
    replies = exchange(fetched.reshape(owners, CAP, width)).reshape(slot_count, width)
    replies = in_vmem(replies)
    weights, part = pl.pallas_call(
        score_kernel,
        out_shape=(
            pltpu.VMEM((question_count, slot_count), jnp.bfloat16),
            pltpu.VMEM((owners, LANES), jnp.float32),
        ),
        in_specs=[VMEM, VMEM, VMEM],
        out_specs=(VMEM, VMEM),
        compiler_params=PARAMS,
        name="score",
    )(questions, replies, info)
    summed = exchange(part)
    grads = pl.pallas_call(
        grads_kernel,
        out_shape=jax.ShapeDtypeStruct((question_count, width), jnp.float32),
        in_specs=[VMEM, VMEM],
        out_specs=VMEM,
        compiler_params=PARAMS,
        name="grads",
    )(weights, replies)
    return (jnp.sum(summed, axis=0)[0], grads)


def solution(mesh):
    placed = P(AXES, None)
    return jax.shard_map(
        body,
        mesh=mesh,
        in_specs=(placed, placed, placed, placed),
        out_specs=(P(), placed),
        check_vma=False,
    )
```

```python
import math

import jax
import jax.numpy as jnp
from jax import lax
from jax.experimental import pallas as pl
from jax.experimental.pallas import tpu as pltpu
from jax.sharding import PartitionSpec as P

AXES = ("index", "bulk")
LANES = 128
CAP = 16
STRIDE = 2048 + 4
STEP = LANES + 4
VMEM = pl.BlockSpec(memory_space=pltpu.VMEM)
HBM = pl.BlockSpec(memory_space=pltpu.HBM)
PARAMS = pltpu.CompilerParams(vmem_limit_bytes=24 << 20)


def in_vmem(array):
    return pltpu.with_memory_space_constraint(array, pltpu.VMEM)


def in_hbm(array):
    return pltpu.with_memory_space_constraint(array, pltpu.HBM)


def exchange(blocks):
    return lax.all_to_all(blocks, AXES, split_axis=0, concat_axis=0, tiled=True)


def log_normalize(logits):
    highest = jnp.max(logits, axis=1, keepdims=True)
    shifted = logits - highest
    return shifted - jnp.log(jnp.sum(jnp.exp(shifted), axis=1, keepdims=True))


def as_lanes(ref):
    return jnp.concatenate([ref[pl.ds(b, 8, stride=4), :] for b in range(4)], axis=1)


def members(owner):
    owners = lax.broadcasted_iota(jnp.int32, (LANES, LANES), 0)
    return [jnp.where(owner[a : a + 1, :] == owners, 1.0, 0.0) for a in range(8)]


def placements(member, values):
    member_low = [m.astype(jnp.bfloat16) for m in member]
    before = lax.broadcasted_iota(jnp.int32, (LANES, 2 * LANES), 0)
    after = lax.broadcasted_iota(jnp.int32, (LANES, 2 * LANES), 1)
    prefix = jnp.where((before < after) | (after >= LANES), 1.0, 0.0).astype(jnp.bfloat16)
    counts = jnp.dot(
        jnp.concatenate(member_low, axis=0), prefix, preferred_element_type=jnp.float32
    )
    slots = lax.broadcasted_iota(jnp.int32, (CAP, LANES), 0).astype(jnp.float32)
    carry = jnp.zeros((LANES, LANES), jnp.float32)
    left = []
    for a in range(8):
        block = counts[a * LANES : (a + 1) * LANES, :]
        rank = jnp.sum(member[a] * (block[:, :LANES] + carry), axis=0, keepdims=True)
        carry = carry + block[:, LANES:]
        here = jnp.where(slots == rank, 1.0, 0.0)
        pieces = [here if v is None else here * v[a : a + 1, :] for v in values]
        left.append(jnp.concatenate(pieces, axis=0).astype(jnp.bfloat16))
    return lax.dot_general(
        jnp.concatenate(left, axis=1),
        jnp.concatenate(member_low, axis=1),
        (((1,), (1,)), ((), ())),
        preferred_element_type=jnp.float32,
    )


def plan_kernel(ids_ref, request_ref):
    ids = as_lanes(ids_ref)
    row = ids & 2047
    high = (row >> 4).astype(jnp.float32)
    low = (row & 15).astype(jnp.float32)
    table = placements(members(ids >> 11), [high, low])
    wanted = (table[:CAP, :] * 16.0 + table[CAP:, :]).astype(jnp.int32)
    padded = jnp.concatenate([wanted, jnp.zeros((LANES - CAP, LANES), jnp.int32)], axis=0)
    request_ref[...] = padded.T


def prepare_kernel(
    ids_hbm, reader_hbm, passages_ref, info_ref, local_ref, ids_ref, reader_scratch, sems
):
    pairs = ((reader_hbm, reader_scratch), (ids_hbm, ids_ref), (passages_ref, local_ref))
    copies = [pltpu.make_async_copy(a, b, sems.at[n]) for n, (a, b) in enumerate(pairs)]
    for copy in copies:
        copy.start()
    copies[0].wait()
    reader_scratch[...] = log_normalize(reader_scratch[...])
    copies[1].wait()
    ids = as_lanes(ids_ref)
    log_reader = as_lanes(reader_scratch)
    question = 4 * lax.broadcasted_iota(jnp.int32, (8, LANES), 0) + (
        lax.broadcasted_iota(jnp.int32, (8, LANES), 1) >> 5
    )
    part0 = log_reader.astype(jnp.bfloat16).astype(jnp.float32)
    rest = log_reader - part0
    part1 = rest.astype(jnp.bfloat16).astype(jnp.float32)
    part2 = rest - part1
    table = placements(
        members(ids >> 11), [(question + 1).astype(jnp.float32), part0, part1, part2]
    )
    owners = lax.broadcasted_iota(jnp.int32, (LANES, LANES * CAP), 0)
    lanes = lax.broadcasted_iota(jnp.int32, (LANES, LANES * CAP), 1)
    spread = jnp.where((lanes >> 4) == owners, 1.0, 0.0).astype(jnp.bfloat16)
    wide = jnp.dot(table.astype(jnp.bfloat16), spread, preferred_element_type=jnp.float32)
    own = (lanes[:CAP] & (CAP - 1)) == owners[:CAP]

    def pick(n):
        return jnp.sum(
            jnp.where(own, wide[n * CAP : (n + 1) * CAP, :], 0.0), axis=0, keepdims=True
        )

    info_ref[...] = jnp.concatenate(
        [
            pick(0) - 1.0,
            pick(1) + pick(2) + pick(3),
            jnp.zeros((6, LANES * CAP), jnp.float32),
        ],
        axis=0,
    )
    copies[2].wait()


def fetch_kernel(wanted_ref, passages_ref, rows_ref, image, even, odd, dense, index, sem):
    count, width = passages_ref.shape
    chunks = width // LANES
    total = jnp.zeros((CAP, LANES), jnp.int32)
    for k in range(8):
        part = wanted_ref[pl.ds(k, 16, stride=8), :]
        total = total + (pltpu.roll(part, CAP * k, 1) if k else part)
    dense[...] = total
    copy = pltpu.make_async_copy(dense, index, sem)
    copy.start()
    for c in range(chunks):
        image[c * STRIDE : c * STRIDE + count, :] = passages_ref[
            :, c * LANES : (c + 1) * LANES
        ].astype(jnp.float32)
    copy.wait()

    def move(line, moved):
        for k in range(LANES):
            r = index[line, k]
            moved[pl.ds(k, chunks, stride=STEP), :] = image[pl.ds(r, chunks, stride=STRIDE), :]

    def pack(line, moved):
        for c in range(chunks):
            rows_ref[line * LANES : (line + 1) * LANES, c * LANES : (c + 1) * LANES] = moved[
                c * STEP : c * STEP + LANES, :
            ].astype(rows_ref.dtype)

    buffers = (even, odd)
    move(0, even)
    for line in range(1, CAP):
        move(line, buffers[line % 2])
        pack(line - 1, buffers[(line - 1) % 2])
    pack(CAP - 1, odd)


def score_kernel(questions_ref, rows_ref, info_ref, logs_ref, part_ref):
    count, width = questions_ref.shape
    scale = 4.0 / math.sqrt(width)
    scores = (
        lax.dot_general(
            questions_ref[...],
            rows_ref[...],
            (((1,), (1,)), ((), ())),
            preferred_element_type=jnp.float32,
        )
        * scale
    )
    question = info_ref[0:1, :]
    log_reader = info_ref[1:2, :]
    mine = question == lax.broadcasted_iota(jnp.int32, scores.shape, 0).astype(jnp.float32)
    highest = jnp.max(jnp.where(mine, scores, -jnp.inf), axis=1, keepdims=True)
    shifted = jnp.where(mine, scores - highest, -jnp.inf)
    log_retriever = shifted - jnp.log(jnp.sum(jnp.exp(shifted), axis=1, keepdims=True))
    reader = jnp.exp(log_reader)
    logs_ref[...] = log_retriever
    own = jnp.sum(jnp.where(mine, log_retriever, 0.0), axis=0, keepdims=True)
    divergence = jnp.where(question >= 0.0, reader * (log_reader - own), 0.0)
    total = jnp.sum(divergence, axis=1, keepdims=True) / (count * part_ref.shape[0])
    part_ref[...] = jnp.broadcast_to(total, part_ref.shape)


def grads_kernel(logs_ref, info_ref, rows_ref, grads_ref):
    scale = 4.0 / math.sqrt(rows_ref.shape[1])
    mine = info_ref[0:1, :] == lax.broadcasted_iota(jnp.int32, logs_ref.shape, 0).astype(
        jnp.float32
    )
    gap = jnp.exp(logs_ref[...]) - jnp.exp(info_ref[1:2, :])
    weights = jnp.where(mine, gap, 0.0).astype(jnp.bfloat16)
    grads_ref[...] = jnp.dot(weights, rows_ref[...], preferred_element_type=jnp.float32) * scale


def body(questions, passages, candidate_ids, reader_loglik):
    owners = lax.axis_size(AXES)
    question_count, width = questions.shape
    slot_count = owners * CAP
    request = pl.pallas_call(
        plan_kernel,
        out_shape=pltpu.VMEM((owners, LANES), jnp.int32),
        in_specs=[VMEM],
        out_specs=VMEM,
        compiler_params=PARAMS,
        name="plan",
    )(candidate_ids)
    wanted = exchange(request)
    info, local = pl.pallas_call(
        prepare_kernel,
        out_shape=(
            pltpu.VMEM((8, slot_count), jnp.float32),
            pltpu.VMEM(passages.shape, passages.dtype),
        ),
        in_specs=[HBM, HBM, HBM],
        out_specs=(VMEM, VMEM),
        scratch_shapes=[
            pltpu.VMEM(candidate_ids.shape, jnp.int32),
            pltpu.VMEM(reader_loglik.shape, jnp.float32),
            pltpu.SemaphoreType.DMA((3,)),
        ],
        compiler_params=PARAMS,
        name="prepare",
    )(in_hbm(candidate_ids), in_hbm(reader_loglik), in_hbm(passages))
    fetched = pl.pallas_call(
        fetch_kernel,
        out_shape=pltpu.VMEM((slot_count, width), passages.dtype),
        in_specs=[VMEM, VMEM],
        out_specs=VMEM,
        scratch_shapes=[
            pltpu.VMEM((width // LANES * STRIDE, LANES), jnp.float32),
            pltpu.VMEM((width // LANES * STEP, LANES), jnp.float32),
            pltpu.VMEM((width // LANES * STEP, LANES), jnp.float32),
            pltpu.VMEM((CAP, LANES), jnp.int32),
            pltpu.SMEM((CAP, LANES), jnp.int32),
            pltpu.SemaphoreType.DMA,
        ],
        compiler_params=PARAMS,
        name="fetch",
    )(wanted, in_vmem(local))
    replies = exchange(fetched.reshape(owners, CAP, width)).reshape(slot_count, width)
    replies = in_vmem(replies)
    logs, part = pl.pallas_call(
        score_kernel,
        out_shape=(
            pltpu.VMEM((question_count, slot_count), jnp.float32),
            pltpu.VMEM((owners, LANES), jnp.float32),
        ),
        in_specs=[VMEM, VMEM, VMEM],
        out_specs=(VMEM, VMEM),
        compiler_params=PARAMS,
        name="score",
    )(questions, replies, info)
    summed = exchange(part)
    grads = pl.pallas_call(
        grads_kernel,
        out_shape=jax.ShapeDtypeStruct((question_count, width), jnp.float32),
        in_specs=[VMEM, VMEM, VMEM],
        out_specs=VMEM,
        compiler_params=PARAMS,
        name="grads",
    )(logs, info, replies)
    return (jnp.sum(summed, axis=0)[0], grads)


def solution(mesh):
    placed = P(AXES, None)
    return jax.shard_map(
        body,
        mesh=mesh,
        in_specs=(placed, placed, placed, placed),
        out_specs=(P(), placed),
        check_vma=False,
    )
```

```python
import math

import jax
import jax.numpy as jnp
from jax import lax
from jax.experimental import pallas as pl
from jax.experimental.pallas import tpu as pltpu
from jax.sharding import PartitionSpec as P

AXES = ("index", "bulk")
LANES = 128
CAP = 16
STRIDE = 2048 + 4
STEP = LANES + 4
VMEM = pl.BlockSpec(memory_space=pltpu.VMEM)
HBM = pl.BlockSpec(memory_space=pltpu.HBM)
PARAMS = pltpu.CompilerParams(vmem_limit_bytes=24 << 20)


def in_vmem(array):
    return pltpu.with_memory_space_constraint(array, pltpu.VMEM)


def in_hbm(array):
    return pltpu.with_memory_space_constraint(array, pltpu.HBM)


def exchange(blocks):
    return lax.all_to_all(blocks, AXES, split_axis=0, concat_axis=0, tiled=True)


def log_normalize(logits):
    highest = jnp.max(logits, axis=1, keepdims=True)
    shifted = logits - highest
    return shifted - jnp.log(jnp.sum(jnp.exp(shifted), axis=1, keepdims=True))


def as_lanes(ref):
    return jnp.concatenate([ref[pl.ds(b, 8, stride=4), :] for b in range(4)], axis=1)


def members(owner):
    owners = lax.broadcasted_iota(jnp.int32, (LANES, LANES), 0)
    return [jnp.where(owner[a : a + 1, :] == owners, 1.0, 0.0) for a in range(8)]


def placements(member, values):
    before = lax.broadcasted_iota(jnp.int32, (LANES, LANES), 0)
    after = lax.broadcasted_iota(jnp.int32, (LANES, LANES), 1)
    prefix = jnp.where(before < after, 1.0, 0.0).astype(jnp.bfloat16)
    above = [jnp.zeros((LANES, LANES), jnp.float32)]
    for m in member:
        above.append(above[-1] + m)
    left_of = jnp.dot(above[8].astype(jnp.bfloat16), prefix, preferred_element_type=jnp.float32)
    places = lax.broadcasted_iota(jnp.int32, (CAP, LANES), 0).astype(jnp.float32)
    left = []
    for a in range(8):
        place = jnp.sum(member[a] * (left_of + above[a]), axis=0, keepdims=True)
        here = jnp.where(places == place, 1.0, 0.0)
        pieces = [here * v[a : a + 1, :] for v in values]
        left.append(jnp.concatenate(pieces, axis=0).astype(jnp.bfloat16))
    return lax.dot_general(
        jnp.concatenate(left, axis=1),
        jnp.concatenate([m.astype(jnp.bfloat16) for m in member], axis=1),
        (((1,), (1,)), ((), ())),
        preferred_element_type=jnp.float32,
    )


def plan_kernel(ids_ref, request_ref):
    ids = as_lanes(ids_ref)
    row = ids & 2047
    high = (row >> 4).astype(jnp.float32)
    low = (row & 15).astype(jnp.float32)
    table = placements(members(ids >> 11), [high, low])
    wanted = (table[:CAP, :] * 16.0 + table[CAP:, :]).astype(jnp.int32)
    padded = jnp.concatenate([wanted, jnp.zeros((LANES - CAP, LANES), jnp.int32)], axis=0)
    request_ref[...] = padded.T


def prepare_kernel(
    ids_hbm, reader_hbm, passages_ref, info_ref, local_ref, ids_ref, reader_scratch, sems
):
    pairs = ((reader_hbm, reader_scratch), (ids_hbm, ids_ref), (passages_ref, local_ref))
    copies = [pltpu.make_async_copy(a, b, sems.at[n]) for n, (a, b) in enumerate(pairs)]
    for copy in copies:
        copy.start()
    copies[0].wait()
    reader_scratch[...] = log_normalize(reader_scratch[...])
    copies[1].wait()
    ids = as_lanes(ids_ref)
    log_reader = as_lanes(reader_scratch)
    number = 4 * lax.broadcasted_iota(jnp.int32, (8, LANES), 0) + (
        lax.broadcasted_iota(jnp.int32, (8, LANES), 1) >> 5
    )
    part0 = log_reader.astype(jnp.bfloat16).astype(jnp.float32)
    rest = log_reader - part0
    part1 = rest.astype(jnp.bfloat16).astype(jnp.float32)
    part2 = rest - part1
    table = placements(
        members(ids >> 11), [(number + 1).astype(jnp.float32), part0, part1, part2]
    )
    owners = lax.broadcasted_iota(jnp.int32, (LANES, LANES * CAP), 0)
    lanes = lax.broadcasted_iota(jnp.int32, (LANES, LANES * CAP), 1)
    spread = jnp.where((lanes >> 4) == owners, 1.0, 0.0).astype(jnp.bfloat16)
    wide = jnp.dot(table.astype(jnp.bfloat16), spread, preferred_element_type=jnp.float32)
    own = (lanes[:CAP] & (CAP - 1)) == owners[:CAP]

    def pick(n):
        return jnp.sum(
            jnp.where(own, wide[n * CAP : (n + 1) * CAP, :], 0.0), axis=0, keepdims=True
        )

    question = pick(0) - 1.0
    log_reader = pick(1) + pick(2) + pick(3)
    reader = jnp.where(question >= 0.0, jnp.exp(log_reader), 0.0)
    rest = jnp.zeros((5, LANES * CAP), jnp.float32)
    info_ref[...] = jnp.concatenate([question, log_reader, reader, rest], axis=0)
    copies[2].wait()


def fetch_kernel(wanted_ref, passages_ref, rows_ref, image, even, odd, dense, index, sem):
    count, width = passages_ref.shape
    chunks = width // LANES
    total = jnp.zeros((CAP, LANES), jnp.int32)
    for k in range(8):
        part = wanted_ref[pl.ds(k, 16, stride=8), :]
        total = total + (pltpu.roll(part, CAP * k, 1) if k else part)
    dense[...] = total
    copy = pltpu.make_async_copy(dense, index, sem)
    copy.start()
    for c in range(chunks):
        image[c * STRIDE : c * STRIDE + count, :] = passages_ref[
            :, c * LANES : (c + 1) * LANES
        ].astype(jnp.float32)
    copy.wait()

    def move(line, moved):
        for k in range(LANES):
            r = index[line, k]
            moved[pl.ds(k, chunks, stride=STEP), :] = image[pl.ds(r, chunks, stride=STRIDE), :]

    def pack(line, moved):
        for c in range(chunks):
            rows_ref[line * LANES : (line + 1) * LANES, c * LANES : (c + 1) * LANES] = moved[
                c * STEP : c * STEP + LANES, :
            ].astype(rows_ref.dtype)

    buffers = (even, odd)
    move(0, even)
    for line in range(1, CAP):
        move(line, buffers[line % 2])
        pack(line - 1, buffers[(line - 1) % 2])
    pack(CAP - 1, odd)


def score_kernel(questions_ref, rows_ref, info_ref, logs_ref, part_ref):
    count, width = questions_ref.shape
    scale = 4.0 / math.sqrt(width)
    scores = (
        lax.dot_general(
            questions_ref[...],
            rows_ref[...],
            (((1,), (1,)), ((), ())),
            preferred_element_type=jnp.float32,
        )
        * scale
    )
    log_reader = info_ref[1:2, :]
    reader = info_ref[2:3, :]
    mine = info_ref[0:1, :] == lax.broadcasted_iota(jnp.int32, scores.shape, 0).astype(jnp.float32)
    masked = jnp.where(mine, scores, -jnp.inf)
    shifted = masked - jnp.max(masked, axis=1, keepdims=True)
    own = jnp.sum(jnp.where(mine, shifted, 0.0), axis=0, keepdims=True)
    known = jnp.sum(reader * (log_reader - own), axis=1, keepdims=True)
    mass = jnp.sum(jnp.where(mine, reader, 0.0), axis=1, keepdims=True)
    log_total = jnp.log(jnp.sum(jnp.exp(shifted), axis=1, keepdims=True))
    logs_ref[...] = shifted - log_total
    divergence = known + jnp.sum(mass * log_total, axis=0, keepdims=True)
    total = divergence / (count * part_ref.shape[0])
    part_ref[...] = jnp.broadcast_to(total, part_ref.shape)


def grads_kernel(logs_ref, info_ref, rows_ref, grads_ref):
    scale = 4.0 / math.sqrt(rows_ref.shape[1])
    mine = info_ref[0:1, :] == lax.broadcasted_iota(jnp.int32, logs_ref.shape, 0).astype(
        jnp.float32
    )
    gap = jnp.exp(logs_ref[...]) - info_ref[2:3, :]
    weights = jnp.where(mine, gap, 0.0).astype(jnp.bfloat16)
    grads_ref[...] = jnp.dot(weights, rows_ref[...], preferred_element_type=jnp.float32) * scale


def body(questions, passages, candidate_ids, reader_loglik):
    owners = lax.axis_size(AXES)
    question_count, width = questions.shape
    slot_count = owners * CAP
    request = pl.pallas_call(
        plan_kernel,
        out_shape=pltpu.VMEM((owners, LANES), jnp.int32),
        in_specs=[VMEM],
        out_specs=VMEM,
        compiler_params=PARAMS,
        name="plan",
    )(candidate_ids)
    wanted = exchange(request)
    info, local = pl.pallas_call(
        prepare_kernel,
        out_shape=(
            pltpu.VMEM((8, slot_count), jnp.float32),
            pltpu.VMEM(passages.shape, passages.dtype),
        ),
        in_specs=[HBM, HBM, HBM],
        out_specs=(VMEM, VMEM),
        scratch_shapes=[
            pltpu.VMEM(candidate_ids.shape, jnp.int32),
            pltpu.VMEM(reader_loglik.shape, jnp.float32),
            pltpu.SemaphoreType.DMA((3,)),
        ],
        compiler_params=PARAMS,
        name="prepare",
    )(in_hbm(candidate_ids), in_hbm(reader_loglik), in_hbm(passages))
    fetched = pl.pallas_call(
        fetch_kernel,
        out_shape=pltpu.VMEM((slot_count, width), passages.dtype),
        in_specs=[VMEM, VMEM],
        out_specs=VMEM,
        scratch_shapes=[
            pltpu.VMEM((width // LANES * STRIDE, LANES), jnp.float32),
            pltpu.VMEM((width // LANES * STEP, LANES), jnp.float32),
            pltpu.VMEM((width // LANES * STEP, LANES), jnp.float32),
            pltpu.VMEM((CAP, LANES), jnp.int32),
            pltpu.SMEM((CAP, LANES), jnp.int32),
            pltpu.SemaphoreType.DMA,
        ],
        compiler_params=PARAMS,
        name="fetch",
    )(wanted, in_vmem(local))
    replies = exchange(fetched.reshape(owners, CAP, width)).reshape(slot_count, width)
    replies = in_vmem(replies)
    logs, part = pl.pallas_call(
        score_kernel,
        out_shape=(
            pltpu.VMEM((question_count, slot_count), jnp.float32),
            pltpu.VMEM((owners, LANES), jnp.float32),
        ),
        in_specs=[VMEM, VMEM, VMEM],
        out_specs=(VMEM, VMEM),
        compiler_params=PARAMS,
        name="score",
    )(questions, replies, info)
    summed = exchange(part)
    grads = pl.pallas_call(
        grads_kernel,
        out_shape=jax.ShapeDtypeStruct((question_count, width), jnp.float32),
        in_specs=[VMEM, VMEM, VMEM],
        out_specs=VMEM,
        compiler_params=PARAMS,
        name="grads",
    )(logs, info, replies)
    return (jnp.sum(summed, axis=0)[0], grads)


def solution(mesh):
    placed = P(AXES, None)
    return jax.shard_map(
        body,
        mesh=mesh,
        in_specs=(placed, placed, placed, placed),
        out_specs=(P(), placed),
        check_vma=False,
    )
```

```python
import math

import jax
import jax.numpy as jnp
from jax import lax
from jax.experimental import pallas as pl
from jax.experimental.pallas import tpu as pltpu
from jax.sharding import PartitionSpec as P

AXES = ("index", "bulk")
LANES = 128
CAP = 16
STRIDE = 2048 + 4
STEP = LANES + 4
VMEM = pl.BlockSpec(memory_space=pltpu.VMEM)
HBM = pl.BlockSpec(memory_space=pltpu.HBM)
PARAMS = pltpu.CompilerParams(vmem_limit_bytes=24 << 20)


def in_vmem(array):
    return pltpu.with_memory_space_constraint(array, pltpu.VMEM)


def in_hbm(array):
    return pltpu.with_memory_space_constraint(array, pltpu.HBM)


def exchange(blocks):
    return lax.all_to_all(blocks, AXES, split_axis=0, concat_axis=0, tiled=True)


def log_normalize(logits):
    highest = jnp.max(logits, axis=1, keepdims=True)
    shifted = logits - highest
    return shifted - jnp.log(jnp.sum(jnp.exp(shifted), axis=1, keepdims=True))


def as_lanes(ref):
    return jnp.concatenate([ref[pl.ds(b, 8, stride=4), :] for b in range(4)], axis=1)


def members(owner):
    owners = lax.broadcasted_iota(jnp.int32, (LANES, LANES), 0)
    return [jnp.where(owner[a : a + 1, :] == owners, 1.0, 0.0) for a in range(8)]


def placements(member, values):
    before = lax.broadcasted_iota(jnp.int32, (LANES, LANES), 0)
    after = lax.broadcasted_iota(jnp.int32, (LANES, LANES), 1)
    prefix = jnp.where(before < after, 1.0, 0.0).astype(jnp.bfloat16)
    above = [jnp.zeros((LANES, LANES), jnp.float32)]
    for m in member:
        above.append(above[-1] + m)
    left_of = jnp.dot(above[8].astype(jnp.bfloat16), prefix, preferred_element_type=jnp.float32)
    places = lax.broadcasted_iota(jnp.int32, (CAP, LANES), 0).astype(jnp.float32)
    left = []
    for a in range(8):
        place = jnp.sum(member[a] * (left_of + above[a]), axis=0, keepdims=True)
        here = jnp.where(places == place, 1.0, 0.0)
        pieces = [here * v[a : a + 1, :] for v in values]
        left.append(jnp.concatenate(pieces, axis=0).astype(jnp.bfloat16))
    return lax.dot_general(
        jnp.concatenate(left, axis=1),
        jnp.concatenate([m.astype(jnp.bfloat16) for m in member], axis=1),
        (((1,), (1,)), ((), ())),
        preferred_element_type=jnp.float32,
    )


def plan_kernel(ids_ref, request_ref):
    ids = as_lanes(ids_ref)
    row = ids & 2047
    high = (row >> 4).astype(jnp.float32)
    low = (row & 15).astype(jnp.float32)
    table = placements(members(ids >> 11), [high, low])
    wanted = (table[:CAP, :] * 16.0 + table[CAP:, :]).astype(jnp.int32)
    padded = jnp.concatenate([wanted, jnp.zeros((LANES - CAP, LANES), jnp.int32)], axis=0)
    request_ref[...] = padded.T


def slot_maps(ids_ref, reader_ref, info_ref, reader_scratch):
    reader_scratch[...] = log_normalize(reader_ref[...])
    ids = as_lanes(ids_ref)
    log_reader = as_lanes(reader_scratch)
    number = 4 * lax.broadcasted_iota(jnp.int32, (8, LANES), 0) + (
        lax.broadcasted_iota(jnp.int32, (8, LANES), 1) >> 5
    )
    part0 = log_reader.astype(jnp.bfloat16).astype(jnp.float32)
    rest = log_reader - part0
    part1 = rest.astype(jnp.bfloat16).astype(jnp.float32)
    part2 = rest - part1
    table = placements(
        members(ids >> 11), [(number + 1).astype(jnp.float32), part0, part1, part2]
    )
    owners = lax.broadcasted_iota(jnp.int32, (LANES, LANES * CAP), 0)
    lanes = lax.broadcasted_iota(jnp.int32, (LANES, LANES * CAP), 1)
    spread = jnp.where((lanes >> 4) == owners, 1.0, 0.0).astype(jnp.bfloat16)
    wide = jnp.dot(table.astype(jnp.bfloat16), spread, preferred_element_type=jnp.float32)
    own = (lanes[:CAP] & (CAP - 1)) == owners[:CAP]

    def pick(n):
        return jnp.sum(
            jnp.where(own, wide[n * CAP : (n + 1) * CAP, :], 0.0), axis=0, keepdims=True
        )

    question = pick(0) - 1.0
    log_reader = pick(1) + pick(2) + pick(3)
    reader = jnp.where(question >= 0.0, jnp.exp(log_reader), 0.0)
    rest = jnp.zeros((5, LANES * CAP), jnp.float32)
    info_ref[...] = jnp.concatenate([question, log_reader, reader, rest], axis=0)


def fetch_kernel(
    wanted_ref,
    passages_ref,
    ids_ref,
    reader_ref,
    rows_ref,
    info_ref,
    image,
    even,
    odd,
    dense,
    reader_scratch,
    index,
    sem,
):
    count, width = passages_ref.shape
    chunks = width // LANES
    total = jnp.zeros((CAP, LANES), jnp.int32)
    for k in range(8):
        part = wanted_ref[pl.ds(k, 16, stride=8), :]
        total = total + (pltpu.roll(part, CAP * k, 1) if k else part)
    dense[...] = total
    copy = pltpu.make_async_copy(dense, index, sem)
    copy.start()
    for c in range(chunks):
        image[c * STRIDE : c * STRIDE + count, :] = passages_ref[
            :, c * LANES : (c + 1) * LANES
        ].astype(jnp.float32)
    slot_maps(ids_ref, reader_ref, info_ref, reader_scratch)
    copy.wait()

    def move(line, moved):
        for k in range(LANES):
            r = index[line, k]
            moved[pl.ds(k, chunks, stride=STEP), :] = image[pl.ds(r, chunks, stride=STRIDE), :]

    def pack(line, moved):
        for c in range(chunks):
            rows_ref[line * LANES : (line + 1) * LANES, c * LANES : (c + 1) * LANES] = moved[
                c * STEP : c * STEP + LANES, :
            ].astype(rows_ref.dtype)

    buffers = (even, odd)
    move(0, even)
    for line in range(1, CAP):
        move(line, buffers[line % 2])
        pack(line - 1, buffers[(line - 1) % 2])
    pack(CAP - 1, odd)


def score_kernel(questions_ref, rows_ref, info_ref, logs_ref, part_ref):
    count, width = questions_ref.shape
    scale = 4.0 / math.sqrt(width)
    scores = (
        lax.dot_general(
            questions_ref[...],
            rows_ref[...],
            (((1,), (1,)), ((), ())),
            preferred_element_type=jnp.float32,
        )
        * scale
    )
    log_reader = info_ref[1:2, :]
    reader = info_ref[2:3, :]
    mine = info_ref[0:1, :] == lax.broadcasted_iota(jnp.int32, scores.shape, 0).astype(jnp.float32)
    masked = jnp.where(mine, scores, -jnp.inf)
    shifted = masked - jnp.max(masked, axis=1, keepdims=True)
    own = jnp.sum(jnp.where(mine, shifted, 0.0), axis=0, keepdims=True)
    known = jnp.sum(reader * (log_reader - own), axis=1, keepdims=True)
    mass = jnp.sum(jnp.where(mine, reader, 0.0), axis=1, keepdims=True)
    log_total = jnp.log(jnp.sum(jnp.exp(shifted), axis=1, keepdims=True))
    logs_ref[...] = shifted - log_total
    divergence = known + jnp.sum(mass * log_total, axis=0, keepdims=True)
    total = divergence / (count * part_ref.shape[0])
    part_ref[...] = jnp.broadcast_to(total, part_ref.shape)


def grads_kernel(logs_ref, info_ref, rows_ref, grads_ref):
    scale = 4.0 / math.sqrt(rows_ref.shape[1])
    mine = info_ref[0:1, :] == lax.broadcasted_iota(jnp.int32, logs_ref.shape, 0).astype(
        jnp.float32
    )
    gap = jnp.exp(logs_ref[...]) - info_ref[2:3, :]
    weights = jnp.where(mine, gap, 0.0).astype(jnp.bfloat16)
    grads_ref[...] = jnp.dot(weights, rows_ref[...], preferred_element_type=jnp.float32) * scale


def body(questions, passages, candidate_ids, reader_loglik):
    owners = lax.axis_size(AXES)
    question_count, width = questions.shape
    slot_count = owners * CAP
    request = pl.pallas_call(
        plan_kernel,
        out_shape=pltpu.VMEM((owners, LANES), jnp.int32),
        in_specs=[VMEM],
        out_specs=VMEM,
        cost_estimate=pl.CostEstimate(flops=1 << 30, transcendentals=0, bytes_accessed=0),
        compiler_params=PARAMS,
        name="plan",
    )(candidate_ids)
    wanted = exchange(request)
    fetched, info = pl.pallas_call(
        fetch_kernel,
        out_shape=(
            pltpu.VMEM((slot_count, width), passages.dtype),
            pltpu.VMEM((8, slot_count), jnp.float32),
        ),
        in_specs=[VMEM, VMEM, VMEM, VMEM],
        out_specs=(VMEM, VMEM),
        scratch_shapes=[
            pltpu.VMEM((width // LANES * STRIDE, LANES), jnp.float32),
            pltpu.VMEM((width // LANES * STEP, LANES), jnp.float32),
            pltpu.VMEM((width // LANES * STEP, LANES), jnp.float32),
            pltpu.VMEM((CAP, LANES), jnp.int32),
            pltpu.VMEM(reader_loglik.shape, jnp.float32),
            pltpu.SMEM((CAP, LANES), jnp.int32),
            pltpu.SemaphoreType.DMA,
        ],
        compiler_params=PARAMS,
        name="fetch",
    )(wanted, in_vmem(passages), in_vmem(candidate_ids), in_vmem(reader_loglik))
    replies = exchange(fetched.reshape(owners, CAP, width)).reshape(slot_count, width)
    replies = in_vmem(replies)
    logs, part = pl.pallas_call(
        score_kernel,
        out_shape=(
            pltpu.VMEM((question_count, slot_count), jnp.float32),
            pltpu.VMEM((owners, LANES), jnp.float32),
        ),
        in_specs=[VMEM, VMEM, VMEM],
        out_specs=(VMEM, VMEM),
        compiler_params=PARAMS,
        name="score",
    )(questions, replies, info)
    summed = exchange(part)
    grads = pl.pallas_call(
        grads_kernel,
        out_shape=jax.ShapeDtypeStruct((question_count, width), jnp.float32),
        in_specs=[VMEM, VMEM, VMEM],
        out_specs=VMEM,
        compiler_params=PARAMS,
        name="grads",
    )(logs, info, replies)
    return (jnp.sum(summed, axis=0)[0], grads)


def solution(mesh):
    placed = P(AXES, None)
    return jax.shard_map(
        body,
        mesh=mesh,
        in_specs=(placed, placed, placed, placed),
        out_specs=(P(), placed),
        check_vma=False,
    )
```

```python
import math

import jax
import jax.numpy as jnp
from jax import lax
from jax.experimental import pallas as pl
from jax.experimental.pallas import tpu as pltpu
from jax.sharding import PartitionSpec as P

AXES = ("index", "bulk")
LANES = 128
CAP = 16
STRIDE = 2048 + 4
STEP = LANES + 4
VMEM = pl.BlockSpec(memory_space=pltpu.VMEM)
HBM = pl.BlockSpec(memory_space=pltpu.HBM)
PARAMS = pltpu.CompilerParams(vmem_limit_bytes=24 << 20)


def in_vmem(array):
    return pltpu.with_memory_space_constraint(array, pltpu.VMEM)


def in_hbm(array):
    return pltpu.with_memory_space_constraint(array, pltpu.HBM)


def exchange(blocks):
    return lax.all_to_all(blocks, AXES, split_axis=0, concat_axis=0, tiled=True)


def log_normalize(logits):
    highest = jnp.max(logits, axis=1, keepdims=True)
    shifted = logits - highest
    return shifted - jnp.log(jnp.sum(jnp.exp(shifted), axis=1, keepdims=True))


def as_lanes(ref):
    return jnp.concatenate([ref[pl.ds(b, 8, stride=4), :] for b in range(4)], axis=1)


def members(owner):
    owners = lax.broadcasted_iota(jnp.int32, (LANES, LANES), 0)
    return [jnp.where(owner[a : a + 1, :] == owners, 1.0, 0.0) for a in range(8)]


def placement_stages(member, values):
    before = lax.broadcasted_iota(jnp.int32, (LANES, LANES), 0)
    after = lax.broadcasted_iota(jnp.int32, (LANES, LANES), 1)
    prefix = jnp.where(before < after, 1.0, 0.0).astype(jnp.bfloat16)
    above = [jnp.zeros((LANES, LANES), jnp.float32)]
    for m in member:
        above.append(above[-1] + m)
    left_of = jnp.dot(above[8].astype(jnp.bfloat16), prefix, preferred_element_type=jnp.float32)
    yield
    places = lax.broadcasted_iota(jnp.int32, (CAP, LANES), 0).astype(jnp.float32)
    left = []
    for a in range(8):
        place = jnp.sum(member[a] * (left_of + above[a]), axis=0, keepdims=True)
        here = jnp.where(places == place, 1.0, 0.0)
        pieces = [here * v[a : a + 1, :] for v in values]
        left.append(jnp.concatenate(pieces, axis=0).astype(jnp.bfloat16))
    yield
    return lax.dot_general(
        jnp.concatenate(left, axis=1),
        jnp.concatenate([m.astype(jnp.bfloat16) for m in member], axis=1),
        (((1,), (1,)), ((), ())),
        preferred_element_type=jnp.float32,
    )


def placements(member, values):
    stages = placement_stages(member, values)
    while True:
        try:
            next(stages)
        except StopIteration as stop:
            return stop.value


def plan_kernel(ids_ref, request_ref, lanes_ref):
    ids = as_lanes(ids_ref)
    lanes_ref[...] = ids
    row = ids & 2047
    high = (row >> 4).astype(jnp.float32)
    low = (row & 15).astype(jnp.float32)
    table = placements(members(ids >> 11), [high, low])
    wanted = (table[:CAP, :] * 16.0 + table[CAP:, :]).astype(jnp.int32)
    padded = jnp.concatenate([wanted, jnp.zeros((LANES - CAP, LANES), jnp.int32)], axis=0)
    request_ref[...] = padded.T


def slot_stages(ids_ref, reader_ref, info_ref, reader_scratch):
    reader_scratch[...] = log_normalize(reader_ref[...])
    yield
    log_reader = as_lanes(reader_scratch)
    number = 4 * lax.broadcasted_iota(jnp.int32, (8, LANES), 0) + (
        lax.broadcasted_iota(jnp.int32, (8, LANES), 1) >> 5
    )
    part0 = log_reader.astype(jnp.bfloat16).astype(jnp.float32)
    rest = log_reader - part0
    part1 = rest.astype(jnp.bfloat16).astype(jnp.float32)
    part2 = rest - part1
    yield
    member = members(ids_ref[...] >> 11)
    yield
    values = [(number + 1).astype(jnp.float32), part0, part1, part2]
    table = yield from placement_stages(member, values)
    table = table.astype(jnp.bfloat16)
    yield
    wide_count = LANES * CAP // 4
    for n in range(4):
        start = n * wide_count
        owners = lax.broadcasted_iota(jnp.int32, (LANES, wide_count), 0)
        lanes = lax.broadcasted_iota(jnp.int32, (LANES, wide_count), 1) + start
        spread = jnp.where((lanes >> 4) == owners, 1.0, 0.0).astype(jnp.bfloat16)
        wide = jnp.dot(table, spread, preferred_element_type=jnp.float32)
        yield
        own = (lanes[:CAP] & (CAP - 1)) == owners[:CAP]
        picked = [
            jnp.sum(jnp.where(own, wide[m * CAP : (m + 1) * CAP, :], 0.0), axis=0, keepdims=True)
            for m in range(4)
        ]
        question = picked[0] - 1.0
        log_part = picked[1] + picked[2] + picked[3]
        reader = jnp.where(question >= 0.0, jnp.exp(log_part), 0.0)
        fill = jnp.zeros((5, wide_count), jnp.float32)
        info_ref[:, start : start + wide_count] = jnp.concatenate(
            [question, log_part, reader, fill], axis=0
        )
        yield


def fetch_kernel(
    wanted_ref,
    passages_ref,
    ids_ref,
    reader_ref,
    rows_ref,
    info_ref,
    image,
    even,
    odd,
    dense,
    reader_scratch,
    index,
    sem,
):
    count, width = passages_ref.shape
    chunks = width // LANES
    total = jnp.zeros((CAP, LANES), jnp.int32)
    for k in range(8):
        part = wanted_ref[pl.ds(k, 16, stride=8), :]
        total = total + (pltpu.roll(part, CAP * k, 1) if k else part)
    dense[...] = total
    copy = pltpu.make_async_copy(dense, index, sem)
    copy.start()
    for c in range(chunks):
        image[c * STRIDE : c * STRIDE + count, :] = passages_ref[
            :, c * LANES : (c + 1) * LANES
        ].astype(jnp.float32)
    stages = slot_stages(ids_ref, reader_ref, info_ref, reader_scratch)
    next(stages)
    copy.wait()

    def move(line, moved):
        for k in range(LANES):
            r = index[line, k]
            moved[pl.ds(k, chunks, stride=STEP), :] = image[pl.ds(r, chunks, stride=STRIDE), :]

    def pack(line, moved):
        for c in range(chunks):
            rows_ref[line * LANES : (line + 1) * LANES, c * LANES : (c + 1) * LANES] = moved[
                c * STEP : c * STEP + LANES, :
            ].astype(rows_ref.dtype)

    buffers = (even, odd)
    move(0, even)
    for line in range(1, CAP):
        move(line, buffers[line % 2])
        next(stages, None)
        pack(line - 1, buffers[(line - 1) % 2])
    for _ in stages:
        pass
    pack(CAP - 1, odd)


def score_kernel(questions_ref, rows_ref, info_ref, logs_ref, part_ref):
    count, width = questions_ref.shape
    scale = 4.0 / math.sqrt(width)
    scores = (
        lax.dot_general(
            questions_ref[...],
            rows_ref[...],
            (((1,), (1,)), ((), ())),
            preferred_element_type=jnp.float32,
        )
        * scale
    )
    log_reader = info_ref[1:2, :]
    reader = info_ref[2:3, :]
    mine = info_ref[0:1, :] == lax.broadcasted_iota(jnp.int32, scores.shape, 0).astype(jnp.float32)
    masked = jnp.where(mine, scores, -jnp.inf)
    shifted = masked - jnp.max(masked, axis=1, keepdims=True)
    own = jnp.sum(jnp.where(mine, shifted, 0.0), axis=0, keepdims=True)
    known = jnp.sum(reader * (log_reader - own), axis=1, keepdims=True)
    mass = jnp.sum(jnp.where(mine, reader, 0.0), axis=1, keepdims=True)
    log_total = jnp.log(jnp.sum(jnp.exp(shifted), axis=1, keepdims=True))
    logs_ref[...] = shifted - log_total
    divergence = known + jnp.sum(mass * log_total, axis=0, keepdims=True)
    total = divergence / (count * part_ref.shape[0])
    part_ref[...] = jnp.broadcast_to(total, part_ref.shape)


def grads_kernel(logs_ref, info_ref, rows_ref, grads_ref):
    scale = 4.0 / math.sqrt(rows_ref.shape[1])
    mine = info_ref[0:1, :] == lax.broadcasted_iota(jnp.int32, logs_ref.shape, 0).astype(
        jnp.float32
    )
    gap = jnp.exp(logs_ref[...]) - info_ref[2:3, :]
    weights = jnp.where(mine, gap, 0.0).astype(jnp.bfloat16)
    grads_ref[...] = jnp.dot(weights, rows_ref[...], preferred_element_type=jnp.float32) * scale


def body(questions, passages, candidate_ids, reader_loglik):
    owners = lax.axis_size(AXES)
    question_count, width = questions.shape
    slot_count = owners * CAP
    request, lanes = pl.pallas_call(
        plan_kernel,
        out_shape=(pltpu.VMEM((owners, LANES), jnp.int32), pltpu.VMEM((8, LANES), jnp.int32)),
        in_specs=[VMEM],
        out_specs=(VMEM, VMEM),
        cost_estimate=pl.CostEstimate(flops=1 << 30, transcendentals=0, bytes_accessed=0),
        compiler_params=PARAMS,
        name="plan",
    )(candidate_ids)
    wanted = exchange(request)
    fetched, info = pl.pallas_call(
        fetch_kernel,
        out_shape=(
            pltpu.VMEM((slot_count, width), passages.dtype),
            pltpu.VMEM((8, slot_count), jnp.float32),
        ),
        in_specs=[VMEM, VMEM, VMEM, VMEM],
        out_specs=(VMEM, VMEM),
        scratch_shapes=[
            pltpu.VMEM((width // LANES * STRIDE, LANES), jnp.float32),
            pltpu.VMEM((width // LANES * STEP, LANES), jnp.float32),
            pltpu.VMEM((width // LANES * STEP, LANES), jnp.float32),
            pltpu.VMEM((CAP, LANES), jnp.int32),
            pltpu.VMEM(reader_loglik.shape, jnp.float32),
            pltpu.SMEM((CAP, LANES), jnp.int32),
            pltpu.SemaphoreType.DMA,
        ],
        compiler_params=PARAMS,
        name="fetch",
    )(wanted, in_vmem(passages), in_vmem(lanes), in_vmem(reader_loglik))
    replies = exchange(fetched.reshape(owners, CAP, width)).reshape(slot_count, width)
    replies = in_vmem(replies)
    logs, part = pl.pallas_call(
        score_kernel,
        out_shape=(
            pltpu.VMEM((question_count, slot_count), jnp.float32),
            pltpu.VMEM((owners, LANES), jnp.float32),
        ),
        in_specs=[VMEM, VMEM, VMEM],
        out_specs=(VMEM, VMEM),
        compiler_params=PARAMS,
        name="score",
    )(questions, replies, info)
    summed = exchange(part)
    grads = pl.pallas_call(
        grads_kernel,
        out_shape=jax.ShapeDtypeStruct((question_count, width), jnp.float32),
        in_specs=[VMEM, VMEM, VMEM],
        out_specs=VMEM,
        compiler_params=PARAMS,
        name="grads",
    )(logs, info, replies)
    return (jnp.sum(summed, axis=0)[0], grads)


def solution(mesh):
    placed = P(AXES, None)
    return jax.shard_map(
        body,
        mesh=mesh,
        in_specs=(placed, placed, placed, placed),
        out_specs=(P(), placed),
        check_vma=False,
    )
```

```python
import math

import jax
import jax.numpy as jnp
from jax import lax
from jax.experimental import pallas as pl
from jax.experimental.pallas import tpu as pltpu
from jax.sharding import PartitionSpec as P

AXES = ("index", "bulk")
LANES = 128
CAP = 16
STRIDE = 2048 + 4
STEP = LANES + 4
VMEM = pl.BlockSpec(memory_space=pltpu.VMEM)
HBM = pl.BlockSpec(memory_space=pltpu.HBM)
PARAMS = pltpu.CompilerParams(vmem_limit_bytes=24 << 20)


def in_vmem(array):
    return pltpu.with_memory_space_constraint(array, pltpu.VMEM)


def in_hbm(array):
    return pltpu.with_memory_space_constraint(array, pltpu.HBM)


def exchange(blocks):
    return lax.all_to_all(blocks, AXES, split_axis=0, concat_axis=0, tiled=True)


def log_normalize(logits):
    highest = jnp.max(logits, axis=1, keepdims=True)
    shifted = logits - highest
    return shifted - jnp.log(jnp.sum(jnp.exp(shifted), axis=1, keepdims=True))


def as_lanes(ref):
    return jnp.concatenate([ref[pl.ds(b, 8, stride=4), :] for b in range(4)], axis=1)


def members(owner):
    owners = lax.broadcasted_iota(jnp.int32, (LANES, LANES), 0)
    return [jnp.where(owner[a : a + 1, :] == owners, 1.0, 0.0) for a in range(8)]


def placement_stages(member, values):
    before = lax.broadcasted_iota(jnp.int32, (LANES, LANES), 0)
    after = lax.broadcasted_iota(jnp.int32, (LANES, LANES), 1)
    prefix = jnp.where(before < after, 1.0, 0.0).astype(jnp.bfloat16)
    above = [jnp.zeros((LANES, LANES), jnp.float32)]
    for m in member:
        above.append(above[-1] + m)
    left_of = jnp.dot(above[8].astype(jnp.bfloat16), prefix, preferred_element_type=jnp.float32)
    yield
    places = lax.broadcasted_iota(jnp.int32, (CAP, LANES), 0).astype(jnp.float32)
    left = []
    for a in range(8):
        place = jnp.sum(member[a] * (left_of + above[a]), axis=0, keepdims=True)
        here = jnp.where(places == place, 1.0, 0.0)
        pieces = [here * v[a : a + 1, :] for v in values]
        left.append(jnp.concatenate(pieces, axis=0).astype(jnp.bfloat16))
    yield
    return lax.dot_general(
        jnp.concatenate(left, axis=1),
        jnp.concatenate([m.astype(jnp.bfloat16) for m in member], axis=1),
        (((1,), (1,)), ((), ())),
        preferred_element_type=jnp.float32,
    )


def placements(member, values):
    stages = placement_stages(member, values)
    while True:
        try:
            next(stages)
        except StopIteration as stop:
            return stop.value


def plan_kernel(ids_ref, request_ref, lanes_ref):
    ids = as_lanes(ids_ref)
    lanes_ref[...] = ids
    row = ids & 2047
    high = (row >> 4).astype(jnp.float32)
    low = (row & 15).astype(jnp.float32)
    table = placements(members(ids >> 11), [high, low])
    wanted = (table[:CAP, :] * 16.0 + table[CAP:, :]).astype(jnp.int32)
    padded = jnp.concatenate([wanted, jnp.zeros((LANES - CAP, LANES), jnp.int32)], axis=0)
    request_ref[...] = padded.T


def slot_stages(ids_ref, reader_ref, info_ref, reader_scratch):
    reader_scratch[...] = log_normalize(reader_ref[...])
    yield
    log_reader = as_lanes(reader_scratch)
    number = 4 * lax.broadcasted_iota(jnp.int32, (8, LANES), 0) + (
        lax.broadcasted_iota(jnp.int32, (8, LANES), 1) >> 5
    )
    part0 = log_reader.astype(jnp.bfloat16).astype(jnp.float32)
    rest = log_reader - part0
    part1 = rest.astype(jnp.bfloat16).astype(jnp.float32)
    part2 = rest - part1
    yield
    member = members(ids_ref[...] >> 11)
    yield
    values = [(number + 1).astype(jnp.float32), part0, part1, part2]
    table = yield from placement_stages(member, values)
    table = table.astype(jnp.bfloat16)
    yield
    wide_count = LANES * CAP // 4
    for n in range(4):
        start = n * wide_count
        owners = lax.broadcasted_iota(jnp.int32, (LANES, wide_count), 0)
        lanes = lax.broadcasted_iota(jnp.int32, (LANES, wide_count), 1) + start
        spread = jnp.where((lanes >> 4) == owners, 1.0, 0.0).astype(jnp.bfloat16)
        wide = jnp.dot(table, spread, preferred_element_type=jnp.float32)
        yield
        own = (lanes[:CAP] & (CAP - 1)) == owners[:CAP]
        picked = [
            jnp.sum(jnp.where(own, wide[m * CAP : (m + 1) * CAP, :], 0.0), axis=0, keepdims=True)
            for m in range(4)
        ]
        question = picked[0] - 1.0
        log_part = picked[1] + picked[2] + picked[3]
        reader = jnp.where(question >= 0.0, jnp.exp(log_part), 0.0)
        fill = jnp.zeros((5, wide_count), jnp.float32)
        info_ref[:, start : start + wide_count] = jnp.concatenate(
            [question, log_part, reader, fill], axis=0
        )
        yield


def fetch_kernel(
    wanted_ref,
    passages_ref,
    ids_ref,
    reader_ref,
    rows_ref,
    info_ref,
    image,
    even,
    odd,
    dense,
    reader_scratch,
    index,
    sem,
):
    count, width = passages_ref.shape
    chunks = width // LANES
    total = jnp.zeros((CAP, LANES), jnp.int32)
    for k in range(8):
        part = wanted_ref[pl.ds(k, 16, stride=8), :]
        total = total + (pltpu.roll(part, CAP * k, 1) if k else part)
    dense[...] = total
    copy = pltpu.make_async_copy(dense, index, sem)
    copy.start()
    for c in range(chunks):
        image[c * STRIDE : c * STRIDE + count, :] = passages_ref[
            :, c * LANES : (c + 1) * LANES
        ].astype(jnp.float32)
    stages = slot_stages(ids_ref, reader_ref, info_ref, reader_scratch)
    next(stages)
    copy.wait()

    def move(line, moved):
        for k in range(LANES):
            r = index[line, k]
            moved[pl.ds(k, chunks, stride=STEP), :] = image[pl.ds(r, chunks, stride=STRIDE), :]

    def pack(line, moved):
        for c in range(chunks):
            rows_ref[line * LANES : (line + 1) * LANES, c * LANES : (c + 1) * LANES] = moved[
                c * STEP : c * STEP + LANES, :
            ].astype(rows_ref.dtype)

    buffers = (even, odd)
    move(0, even)
    for line in range(1, CAP):
        move(line, buffers[line % 2])
        next(stages, None)
        pack(line - 1, buffers[(line - 1) % 2])
    for _ in stages:
        pass
    pack(CAP - 1, odd)


def score_kernel(questions_ref, rows_ref, info_ref, grads_ref, part_ref):
    count, width = questions_ref.shape
    scale = 4.0 / math.sqrt(width)
    scores = (
        lax.dot_general(
            questions_ref[...],
            rows_ref[...],
            (((1,), (1,)), ((), ())),
            preferred_element_type=jnp.float32,
        )
        * scale
    )
    log_reader = info_ref[1:2, :]
    reader = info_ref[2:3, :]
    mine = info_ref[0:1, :] == lax.broadcasted_iota(jnp.int32, scores.shape, 0).astype(jnp.float32)
    masked = jnp.where(mine, scores, -jnp.inf)
    shifted = masked - jnp.max(masked, axis=1, keepdims=True)
    own = jnp.sum(jnp.where(mine, shifted, 0.0), axis=0, keepdims=True)
    known = jnp.sum(reader * (log_reader - own), axis=1, keepdims=True)
    mass = jnp.sum(jnp.where(mine, reader, 0.0), axis=1, keepdims=True)
    log_total = jnp.log(jnp.sum(jnp.exp(shifted), axis=1, keepdims=True))
    weights = jnp.where(mine, jnp.exp(shifted - log_total) - reader, 0.0).astype(jnp.bfloat16)
    grads_ref[...] = jnp.dot(weights, rows_ref[...], preferred_element_type=jnp.float32) * scale
    divergence = known + jnp.sum(mass * log_total, axis=0, keepdims=True)
    total = divergence / (count * part_ref.shape[0])
    part_ref[...] = jnp.broadcast_to(total, part_ref.shape)


def finish_kernel(sums_ref, local_ref, mean_ref, grads_ref):
    grads_ref[...] = local_ref[...]
    mean_ref[...] = jnp.sum(sums_ref[...], axis=0, keepdims=True)[:, :1]


def body(questions, passages, candidate_ids, reader_loglik):
    owners = lax.axis_size(AXES)
    question_count, width = questions.shape
    slot_count = owners * CAP
    request, lanes = pl.pallas_call(
        plan_kernel,
        out_shape=(pltpu.VMEM((owners, LANES), jnp.int32), pltpu.VMEM((8, LANES), jnp.int32)),
        in_specs=[VMEM],
        out_specs=(VMEM, VMEM),
        cost_estimate=pl.CostEstimate(flops=1 << 30, transcendentals=0, bytes_accessed=0),
        compiler_params=PARAMS,
        name="plan",
    )(candidate_ids)
    wanted = exchange(request)
    fetched, info = pl.pallas_call(
        fetch_kernel,
        out_shape=(
            pltpu.VMEM((slot_count, width), passages.dtype),
            pltpu.VMEM((8, slot_count), jnp.float32),
        ),
        in_specs=[VMEM, VMEM, VMEM, VMEM],
        out_specs=(VMEM, VMEM),
        scratch_shapes=[
            pltpu.VMEM((width // LANES * STRIDE, LANES), jnp.float32),
            pltpu.VMEM((width // LANES * STEP, LANES), jnp.float32),
            pltpu.VMEM((width // LANES * STEP, LANES), jnp.float32),
            pltpu.VMEM((CAP, LANES), jnp.int32),
            pltpu.VMEM(reader_loglik.shape, jnp.float32),
            pltpu.SMEM((CAP, LANES), jnp.int32),
            pltpu.SemaphoreType.DMA,
        ],
        compiler_params=PARAMS,
        name="fetch",
    )(wanted, in_vmem(passages), in_vmem(lanes), in_vmem(reader_loglik))
    replies = exchange(fetched.reshape(owners, CAP, width)).reshape(slot_count, width)
    replies = in_vmem(replies)
    grads, part = pl.pallas_call(
        score_kernel,
        out_shape=(
            pltpu.VMEM((question_count, width), jnp.float32),
            pltpu.VMEM((owners, LANES), jnp.float32),
        ),
        in_specs=[VMEM, VMEM, VMEM],
        out_specs=(VMEM, VMEM),
        compiler_params=PARAMS,
        name="score",
    )(questions, replies, info)
    mean, out = pl.pallas_call(
        finish_kernel,
        out_shape=(
            jax.ShapeDtypeStruct((1, 1), jnp.float32),
            jax.ShapeDtypeStruct((question_count, width), jnp.float32),
        ),
        in_specs=[VMEM, VMEM],
        out_specs=(VMEM, VMEM),
        compiler_params=PARAMS,
        name="finish",
    )(exchange(part), in_vmem(grads))
    return (mean.reshape(()), out)


def solution(mesh):
    placed = P(AXES, None)
    return jax.shard_map(
        body,
        mesh=mesh,
        in_specs=(placed, placed, placed, placed),
        out_specs=(P(), placed),
        check_vma=False,
    )
```

```python
import math

import jax
import jax.numpy as jnp
from jax import lax
from jax.experimental import pallas as pl
from jax.experimental.pallas import tpu as pltpu
from jax.sharding import PartitionSpec as P

AXES = ("index", "bulk")
LANES = 128
CAP = 16
STRIDE = 2048 + 4
STEP = LANES + 4
VMEM = pl.BlockSpec(memory_space=pltpu.VMEM)
HBM = pl.BlockSpec(memory_space=pltpu.HBM)
PARAMS = pltpu.CompilerParams(vmem_limit_bytes=24 << 20)


def in_vmem(array):
    return pltpu.with_memory_space_constraint(array, pltpu.VMEM)


def in_hbm(array):
    return pltpu.with_memory_space_constraint(array, pltpu.HBM)


def exchange(blocks):
    return lax.all_to_all(blocks, AXES, split_axis=0, concat_axis=0, tiled=True)


def log_normalize(logits):
    highest = jnp.max(logits, axis=1, keepdims=True)
    shifted = logits - highest
    return shifted - jnp.log(jnp.sum(jnp.exp(shifted), axis=1, keepdims=True))


def as_lanes(ref):
    return jnp.concatenate([ref[pl.ds(b, 8, stride=4), :] for b in range(4)], axis=1)


def members(owner):
    owners = lax.broadcasted_iota(jnp.int32, (LANES, LANES), 0)
    return [jnp.where(owner[a : a + 1, :] == owners, 1.0, 0.0) for a in range(8)]


def placement_stages(member, values):
    before = lax.broadcasted_iota(jnp.int32, (LANES, LANES), 0)
    after = lax.broadcasted_iota(jnp.int32, (LANES, LANES), 1)
    prefix = jnp.where(before < after, 1.0, 0.0).astype(jnp.bfloat16)
    above = [jnp.zeros((LANES, LANES), jnp.float32)]
    for m in member:
        above.append(above[-1] + m)
    left_of = jnp.dot(above[8].astype(jnp.bfloat16), prefix, preferred_element_type=jnp.float32)
    yield
    places = lax.broadcasted_iota(jnp.int32, (CAP, LANES), 0).astype(jnp.float32)
    left = []
    for a in range(8):
        place = jnp.sum(member[a] * (left_of + above[a]), axis=0, keepdims=True)
        here = jnp.where(places == place, 1.0, 0.0)
        pieces = [here * v[a : a + 1, :] for v in values]
        left.append(jnp.concatenate(pieces, axis=0).astype(jnp.bfloat16))
    yield
    return lax.dot_general(
        jnp.concatenate(left, axis=1),
        jnp.concatenate([m.astype(jnp.bfloat16) for m in member], axis=1),
        (((1,), (1,)), ((), ())),
        preferred_element_type=jnp.float32,
    )


def placements(member, values):
    stages = placement_stages(member, values)
    while True:
        try:
            next(stages)
        except StopIteration as stop:
            return stop.value


def plan_kernel(ids_ref, request_ref, lanes_ref):
    ids = as_lanes(ids_ref)
    lanes_ref[...] = ids
    row = ids & 2047
    high = (row >> 4).astype(jnp.float32)
    low = (row & 15).astype(jnp.float32)
    table = placements(members(ids >> 11), [high, low])
    wanted = (table[:CAP, :] * 16.0 + table[CAP:, :]).astype(jnp.int32)
    padded = jnp.concatenate([wanted, jnp.zeros((LANES - CAP, LANES), jnp.int32)], axis=0)
    request_ref[...] = padded.T


def slot_stages(ids_ref, reader_ref, info_ref, reader_scratch):
    reader_scratch[...] = log_normalize(reader_ref[...])
    yield
    log_reader = as_lanes(reader_scratch)
    number = 4 * lax.broadcasted_iota(jnp.int32, (8, LANES), 0) + (
        lax.broadcasted_iota(jnp.int32, (8, LANES), 1) >> 5
    )
    part0 = log_reader.astype(jnp.bfloat16).astype(jnp.float32)
    rest = log_reader - part0
    part1 = rest.astype(jnp.bfloat16).astype(jnp.float32)
    part2 = rest - part1
    yield
    member = members(ids_ref[...] >> 11)
    yield
    values = [(number + 1).astype(jnp.float32), part0, part1, part2]
    table = yield from placement_stages(member, values)
    table = table.astype(jnp.bfloat16)
    yield
    wide_count = LANES * CAP // 4
    for n in range(4):
        start = n * wide_count
        owners = lax.broadcasted_iota(jnp.int32, (LANES, wide_count), 0)
        lanes = lax.broadcasted_iota(jnp.int32, (LANES, wide_count), 1) + start
        spread = jnp.where((lanes >> 4) == owners, 1.0, 0.0).astype(jnp.bfloat16)
        wide = jnp.dot(table, spread, preferred_element_type=jnp.float32)
        yield
        own = (lanes[:CAP] & (CAP - 1)) == owners[:CAP]
        picked = [
            jnp.sum(jnp.where(own, wide[m * CAP : (m + 1) * CAP, :], 0.0), axis=0, keepdims=True)
            for m in range(4)
        ]
        question = picked[0] - 1.0
        log_part = picked[1] + picked[2] + picked[3]
        reader = jnp.where(question >= 0.0, jnp.exp(log_part), 0.0)
        fill = jnp.zeros((5, wide_count), jnp.float32)
        info_ref[:, start : start + wide_count] = jnp.concatenate(
            [question, log_part, reader, fill], axis=0
        )
        yield


def fetch_kernel(
    wanted_ref,
    passages_ref,
    ids_ref,
    reader_ref,
    rows_ref,
    info_ref,
    image,
    even,
    odd,
    dense,
    reader_scratch,
    index,
    sem,
):
    count, width = passages_ref.shape
    chunks = width // LANES
    total = jnp.zeros((CAP, LANES), jnp.int32)
    for k in range(8):
        part = wanted_ref[pl.ds(k, 16, stride=8), :]
        total = total + (pltpu.roll(part, CAP * k, 1) if k else part)
    dense[...] = total
    copy = pltpu.make_async_copy(dense, index, sem)
    copy.start()
    for c in range(chunks):
        image[c * STRIDE : c * STRIDE + count, :] = passages_ref[
            :, c * LANES : (c + 1) * LANES
        ].astype(jnp.float32)
    stages = slot_stages(ids_ref, reader_ref, info_ref, reader_scratch)
    next(stages)
    copy.wait()

    def move(line, moved):
        for k in range(LANES):
            r = index[line, k]
            moved[pl.ds(k, chunks, stride=STEP), :] = image[pl.ds(r, chunks, stride=STRIDE), :]

    def pack(line, moved):
        for c in range(chunks):
            rows_ref[line * LANES : (line + 1) * LANES, c * LANES : (c + 1) * LANES] = moved[
                c * STEP : c * STEP + LANES, :
            ].astype(rows_ref.dtype)

    buffers = (even, odd)
    move(0, even)
    for line in range(1, CAP):
        move(line, buffers[line % 2])
        next(stages, None)
        pack(line - 1, buffers[(line - 1) % 2])
    for _ in stages:
        pass
    pack(CAP - 1, odd)


def inner(left, right):
    return lax.dot_general(
        left, right, (((1,), (1,)), ((), ())), preferred_element_type=jnp.float32
    )


def score_kernel(questions_ref, rows_ref, info_ref, weights_ref, part_ref):
    count, width = questions_ref.shape
    scale = 4.0 / math.sqrt(width)
    questions = questions_ref[...]
    block = rows_ref.shape[0] // 8
    pieces = []
    for n in range(8):
        rows = rows_ref[n * block : (n + 1) * block, :]
        pieces.append(inner(rows, questions).T if n % 2 else inner(questions, rows))
    scores = jnp.concatenate(pieces, axis=1) * scale
    log_reader = info_ref[1:2, :]
    reader = info_ref[2:3, :]
    mine = info_ref[0:1, :] == lax.broadcasted_iota(jnp.int32, scores.shape, 0).astype(jnp.float32)
    masked = jnp.where(mine, scores, -jnp.inf)
    shifted = masked - jnp.max(masked, axis=1, keepdims=True)
    own = jnp.sum(jnp.where(mine, shifted, 0.0), axis=0, keepdims=True)
    known = jnp.sum(reader * (log_reader - own), axis=1, keepdims=True)
    mass = jnp.sum(jnp.where(mine, reader, 0.0), axis=1, keepdims=True)
    log_total = jnp.log(jnp.sum(jnp.exp(shifted), axis=1, keepdims=True))
    gap = jnp.exp(shifted - log_total) - reader
    weights_ref[...] = jnp.where(mine, gap, 0.0).astype(jnp.bfloat16)
    divergence = known + jnp.sum(mass * log_total, axis=0, keepdims=True)
    total = divergence / (count * part_ref.shape[0])
    part_ref[...] = jnp.broadcast_to(total, part_ref.shape)


def finish_kernel(sums_ref, weights_ref, rows_ref, mean_ref, grads_ref):
    scale = 4.0 / math.sqrt(rows_ref.shape[1])
    mean_ref[...] = jnp.sum(sums_ref[...], axis=0, keepdims=True)[:, :1]
    grads_ref[...] = (
        jnp.dot(weights_ref[...], rows_ref[...], preferred_element_type=jnp.float32) * scale
    )


def body(questions, passages, candidate_ids, reader_loglik):
    owners = lax.axis_size(AXES)
    question_count, width = questions.shape
    slot_count = owners * CAP
    request, lanes = pl.pallas_call(
        plan_kernel,
        out_shape=(pltpu.VMEM((owners, LANES), jnp.int32), pltpu.VMEM((8, LANES), jnp.int32)),
        in_specs=[VMEM],
        out_specs=(VMEM, VMEM),
        cost_estimate=pl.CostEstimate(flops=1 << 30, transcendentals=0, bytes_accessed=0),
        compiler_params=PARAMS,
        name="plan",
    )(candidate_ids)
    wanted = exchange(request)
    fetched, info = pl.pallas_call(
        fetch_kernel,
        out_shape=(
            pltpu.VMEM((slot_count, width), passages.dtype),
            pltpu.VMEM((8, slot_count), jnp.float32),
        ),
        in_specs=[VMEM, VMEM, VMEM, VMEM],
        out_specs=(VMEM, VMEM),
        scratch_shapes=[
            pltpu.VMEM((width // LANES * STRIDE, LANES), jnp.float32),
            pltpu.VMEM((width // LANES * STEP, LANES), jnp.float32),
            pltpu.VMEM((width // LANES * STEP, LANES), jnp.float32),
            pltpu.VMEM((CAP, LANES), jnp.int32),
            pltpu.VMEM(reader_loglik.shape, jnp.float32),
            pltpu.SMEM((CAP, LANES), jnp.int32),
            pltpu.SemaphoreType.DMA,
        ],
        compiler_params=PARAMS,
        name="fetch",
    )(wanted, in_vmem(passages), in_vmem(lanes), in_vmem(reader_loglik))
    replies = exchange(fetched.reshape(owners, CAP, width)).reshape(slot_count, width)
    replies = in_vmem(replies)
    weights, part = pl.pallas_call(
        score_kernel,
        out_shape=(
            pltpu.VMEM((question_count, slot_count), jnp.bfloat16),
            pltpu.VMEM((owners, LANES), jnp.float32),
        ),
        in_specs=[VMEM, VMEM, VMEM],
        out_specs=(VMEM, VMEM),
        compiler_params=PARAMS,
        name="score",
    )(questions, replies, info)
    mean, grads = pl.pallas_call(
        finish_kernel,
        out_shape=(
            jax.ShapeDtypeStruct((1, 1), jnp.float32),
            jax.ShapeDtypeStruct((question_count, width), jnp.float32),
        ),
        in_specs=[VMEM, VMEM, VMEM],
        out_specs=(VMEM, VMEM),
        compiler_params=PARAMS,
        name="finish",
    )(exchange(part), weights, replies)
    return (mean.reshape(()), grads)


def solution(mesh):
    placed = P(AXES, None)
    return jax.shard_map(
        body,
        mesh=mesh,
        in_specs=(placed, placed, placed, placed),
        out_specs=(P(), placed),
        check_vma=False,
    )
```

```python
import math

import jax
import jax.numpy as jnp
from jax import lax
from jax.experimental import pallas as pl
from jax.experimental.pallas import tpu as pltpu
from jax.sharding import PartitionSpec as P

AXES = ("index", "bulk")
LANES = 128
CAP = 16
STRIDE = 2048 + 4
STEP = LANES + 4
VMEM = pl.BlockSpec(memory_space=pltpu.VMEM)
HBM = pl.BlockSpec(memory_space=pltpu.HBM)
PARAMS = pltpu.CompilerParams(vmem_limit_bytes=24 << 20)


def in_vmem(array):
    return pltpu.with_memory_space_constraint(array, pltpu.VMEM)


def in_hbm(array):
    return pltpu.with_memory_space_constraint(array, pltpu.HBM)


def exchange(blocks):
    return lax.all_to_all(blocks, AXES, split_axis=0, concat_axis=0, tiled=True)


def log_normalize(logits):
    highest = jnp.max(logits, axis=1, keepdims=True)
    shifted = logits - highest
    return shifted - jnp.log(jnp.sum(jnp.exp(shifted), axis=1, keepdims=True))


def as_lanes(ref):
    return jnp.concatenate([ref[pl.ds(b, 8, stride=4), :] for b in range(4)], axis=1)


def members(owner):
    owners = lax.broadcasted_iota(jnp.int32, (LANES, LANES), 0)
    return [jnp.where(owner[a : a + 1, :] == owners, 1.0, 0.0) for a in range(8)]


def place_onehots(member):
    before = lax.broadcasted_iota(jnp.int32, (LANES, LANES), 0)
    after = lax.broadcasted_iota(jnp.int32, (LANES, LANES), 1)
    prefix = jnp.where(before < after, 1.0, 0.0).astype(jnp.bfloat16)
    above = [jnp.zeros((LANES, LANES), jnp.float32)]
    for m in member:
        above.append(above[-1] + m)
    left_of = jnp.dot(above[8].astype(jnp.bfloat16), prefix, preferred_element_type=jnp.float32)
    places = lax.broadcasted_iota(jnp.int32, (CAP, LANES), 0).astype(jnp.float32)
    onehots = []
    for a in range(8):
        place = jnp.sum(member[a] * (left_of + above[a]), axis=0, keepdims=True)
        onehots.append(jnp.where(places == place, 1.0, 0.0))
    return onehots


def placed(member, onehots, values):
    left = []
    for a in range(8):
        pieces = [onehots[a] * v[a : a + 1, :] for v in values]
        left.append(jnp.concatenate(pieces, axis=0).astype(jnp.bfloat16))
    return lax.dot_general(
        jnp.concatenate(left, axis=1),
        jnp.concatenate([m.astype(jnp.bfloat16) for m in member], axis=1),
        (((1,), (1,)), ((), ())),
        preferred_element_type=jnp.float32,
    )


def plan_kernel(ids_ref, request_ref, lanes_ref, places_ref):
    ids = as_lanes(ids_ref)
    lanes_ref[...] = ids
    row = ids & 2047
    high = (row >> 4).astype(jnp.float32)
    low = (row & 15).astype(jnp.float32)
    member = members(ids >> 11)
    onehots = place_onehots(member)
    for a in range(8):
        places_ref[a * CAP : (a + 1) * CAP, :] = onehots[a]
    table = placed(member, onehots, [high, low])
    wanted = (table[:CAP, :] * 16.0 + table[CAP:, :]).astype(jnp.int32)
    padded = jnp.concatenate([wanted, jnp.zeros((LANES - CAP, LANES), jnp.int32)], axis=0)
    request_ref[...] = padded.T


def slot_stages(ids_ref, places_ref, reader_ref, info_ref, reader_scratch):
    reader_scratch[...] = log_normalize(reader_ref[...])
    yield
    log_reader = as_lanes(reader_scratch)
    number = 4 * lax.broadcasted_iota(jnp.int32, (8, LANES), 0) + (
        lax.broadcasted_iota(jnp.int32, (8, LANES), 1) >> 5
    )
    part0 = log_reader.astype(jnp.bfloat16).astype(jnp.float32)
    rest = log_reader - part0
    part1 = rest.astype(jnp.bfloat16).astype(jnp.float32)
    part2 = rest - part1
    yield
    member = members(ids_ref[...] >> 11)
    yield
    values = [(number + 1).astype(jnp.float32), part0, part1, part2]
    onehots = [places_ref[a * CAP : (a + 1) * CAP, :] for a in range(8)]
    table = placed(member, onehots, values).astype(jnp.bfloat16)
    yield
    wide_count = LANES * CAP // 4
    for n in range(4):
        start = n * wide_count
        owners = lax.broadcasted_iota(jnp.int32, (LANES, wide_count), 0)
        lanes = lax.broadcasted_iota(jnp.int32, (LANES, wide_count), 1) + start
        spread = jnp.where((lanes >> 4) == owners, 1.0, 0.0).astype(jnp.bfloat16)
        wide = jnp.dot(table, spread, preferred_element_type=jnp.float32)
        yield
        own = (lanes[:CAP] & (CAP - 1)) == owners[:CAP]
        picked = [
            jnp.sum(jnp.where(own, wide[m * CAP : (m + 1) * CAP, :], 0.0), axis=0, keepdims=True)
            for m in range(4)
        ]
        question = picked[0] - 1.0
        log_part = picked[1] + picked[2] + picked[3]
        reader = jnp.where(question >= 0.0, jnp.exp(log_part), 0.0)
        fill = jnp.zeros((5, wide_count), jnp.float32)
        info_ref[:, start : start + wide_count] = jnp.concatenate(
            [question, log_part, reader, fill], axis=0
        )
        yield


def fetch_kernel(
    wanted_ref,
    passages_ref,
    ids_ref,
    places_ref,
    reader_ref,
    rows_ref,
    info_ref,
    image,
    even,
    odd,
    dense,
    reader_scratch,
    index,
    sem,
):
    count, width = passages_ref.shape
    chunks = width // LANES
    total = jnp.zeros((CAP, LANES), jnp.int32)
    for k in range(8):
        part = wanted_ref[pl.ds(k, 16, stride=8), :]
        total = total + (pltpu.roll(part, CAP * k, 1) if k else part)
    dense[...] = total
    copy = pltpu.make_async_copy(dense, index, sem)
    copy.start()
    for c in range(chunks):
        image[c * STRIDE : c * STRIDE + count, :] = passages_ref[
            :, c * LANES : (c + 1) * LANES
        ].astype(jnp.float32)
    stages = slot_stages(ids_ref, places_ref, reader_ref, info_ref, reader_scratch)
    next(stages)
    copy.wait()

    def move(line, moved):
        for k in range(LANES):
            r = index[line, k]
            moved[pl.ds(k, chunks, stride=STEP), :] = image[pl.ds(r, chunks, stride=STRIDE), :]

    def pack(line, moved):
        for c in range(chunks):
            rows_ref[line * LANES : (line + 1) * LANES, c * LANES : (c + 1) * LANES] = moved[
                c * STEP : c * STEP + LANES, :
            ].astype(rows_ref.dtype)

    buffers = (even, odd)
    move(0, even)
    for line in range(1, CAP):
        move(line, buffers[line % 2])
        next(stages, None)
        pack(line - 1, buffers[(line - 1) % 2])
    for _ in stages:
        pass
    pack(CAP - 1, odd)


def inner(left, right):
    return lax.dot_general(
        left, right, (((1,), (1,)), ((), ())), preferred_element_type=jnp.float32
    )


def score_kernel(questions_ref, rows_ref, info_ref, weights_ref, part_ref):
    count, width = questions_ref.shape
    scale = 4.0 / math.sqrt(width)
    questions = questions_ref[...]
    block = rows_ref.shape[0] // 8
    pieces = []
    for n in range(8):
        rows = rows_ref[n * block : (n + 1) * block, :]
        pieces.append(inner(rows, questions).T if n % 2 else inner(questions, rows))
    scores = jnp.concatenate(pieces, axis=1) * scale
    log_reader = info_ref[1:2, :]
    reader = info_ref[2:3, :]
    mine = info_ref[0:1, :] == lax.broadcasted_iota(jnp.int32, scores.shape, 0).astype(jnp.float32)
    masked = jnp.where(mine, scores, -jnp.inf)
    shifted = masked - jnp.max(masked, axis=1, keepdims=True)
    own = jnp.sum(jnp.where(mine, shifted, 0.0), axis=0, keepdims=True)
    known = jnp.sum(reader * (log_reader - own), axis=1, keepdims=True)
    mass = jnp.sum(jnp.where(mine, reader, 0.0), axis=1, keepdims=True)
    log_total = jnp.log(jnp.sum(jnp.exp(shifted), axis=1, keepdims=True))
    gap = jnp.exp(shifted - log_total) - reader
    weights_ref[...] = jnp.where(mine, gap, 0.0).astype(jnp.bfloat16)
    divergence = known + jnp.sum(mass * log_total, axis=0, keepdims=True)
    total = divergence / (count * part_ref.shape[0])
    part_ref[...] = jnp.broadcast_to(total, part_ref.shape)


def finish_kernel(sums_ref, weights_ref, rows_ref, mean_ref, grads_ref):
    scale = 4.0 / math.sqrt(rows_ref.shape[1])
    mean_ref[...] = jnp.sum(sums_ref[...], axis=0, keepdims=True)[:, :1]
    grads_ref[...] = (
        jnp.dot(weights_ref[...], rows_ref[...], preferred_element_type=jnp.float32) * scale
    )


def body(questions, passages, candidate_ids, reader_loglik):
    owners = lax.axis_size(AXES)
    question_count, width = questions.shape
    slot_count = owners * CAP
    request, lanes, places = pl.pallas_call(
        plan_kernel,
        out_shape=(
            pltpu.VMEM((owners, LANES), jnp.int32),
            pltpu.VMEM((8, LANES), jnp.int32),
            pltpu.VMEM((8 * CAP, LANES), jnp.float32),
        ),
        in_specs=[VMEM],
        out_specs=(VMEM, VMEM, VMEM),
        cost_estimate=pl.CostEstimate(flops=1 << 30, transcendentals=0, bytes_accessed=0),
        compiler_params=PARAMS,
        name="plan",
    )(candidate_ids)
    wanted = exchange(request)
    fetched, info = pl.pallas_call(
        fetch_kernel,
        out_shape=(
            pltpu.VMEM((slot_count, width), passages.dtype),
            pltpu.VMEM((8, slot_count), jnp.float32),
        ),
        in_specs=[VMEM, VMEM, VMEM, VMEM, VMEM],
        out_specs=(VMEM, VMEM),
        scratch_shapes=[
            pltpu.VMEM((width // LANES * STRIDE, LANES), jnp.float32),
            pltpu.VMEM((width // LANES * STEP, LANES), jnp.float32),
            pltpu.VMEM((width // LANES * STEP, LANES), jnp.float32),
            pltpu.VMEM((CAP, LANES), jnp.int32),
            pltpu.VMEM(reader_loglik.shape, jnp.float32),
            pltpu.SMEM((CAP, LANES), jnp.int32),
            pltpu.SemaphoreType.DMA,
        ],
        compiler_params=PARAMS,
        name="fetch",
    )(wanted, in_vmem(passages), in_vmem(lanes), in_vmem(places), in_vmem(reader_loglik))
    replies = exchange(fetched.reshape(owners, CAP, width)).reshape(slot_count, width)
    replies = in_vmem(replies)
    weights, part = pl.pallas_call(
        score_kernel,
        out_shape=(
            pltpu.VMEM((question_count, slot_count), jnp.bfloat16),
            pltpu.VMEM((owners, LANES), jnp.float32),
        ),
        in_specs=[VMEM, VMEM, VMEM],
        out_specs=(VMEM, VMEM),
        compiler_params=PARAMS,
        name="score",
    )(questions, replies, info)
    mean, grads = pl.pallas_call(
        finish_kernel,
        out_shape=(
            jax.ShapeDtypeStruct((1, 1), jnp.float32),
            jax.ShapeDtypeStruct((question_count, width), jnp.float32),
        ),
        in_specs=[VMEM, VMEM, VMEM],
        out_specs=(VMEM, VMEM),
        compiler_params=PARAMS,
        name="finish",
    )(exchange(part), weights, replies)
    return (mean.reshape(()), grads)


def solution(mesh):
    placed = P(AXES, None)
    return jax.shard_map(
        body,
        mesh=mesh,
        in_specs=(placed, placed, placed, placed),
        out_specs=(P(), placed),
        check_vma=False,
    )
```

```python
import math

import jax
import jax.numpy as jnp
from jax import lax
from jax.experimental import pallas as pl
from jax.experimental.pallas import tpu as pltpu
from jax.sharding import PartitionSpec as P

AXES = ("index", "bulk")
LANES = 128
CAP = 16
STRIDE = 2048 + 4
STEP = LANES + 4
VMEM = pl.BlockSpec(memory_space=pltpu.VMEM)
HBM = pl.BlockSpec(memory_space=pltpu.HBM)
PARAMS = pltpu.CompilerParams(vmem_limit_bytes=24 << 20)


def in_vmem(array):
    return pltpu.with_memory_space_constraint(array, pltpu.VMEM)


def in_hbm(array):
    return pltpu.with_memory_space_constraint(array, pltpu.HBM)


def exchange(blocks):
    return lax.all_to_all(blocks, AXES, split_axis=0, concat_axis=0, tiled=True)


def log_normalize(logits):
    highest = jnp.max(logits, axis=1, keepdims=True)
    shifted = logits - highest
    return shifted - jnp.log(jnp.sum(jnp.exp(shifted), axis=1, keepdims=True))


def as_lanes(ref):
    return jnp.concatenate([ref[pl.ds(b, 8, stride=4), :] for b in range(4)], axis=1)


def members(owner):
    owners = lax.broadcasted_iota(jnp.int32, (LANES, LANES), 0)
    return [jnp.where(owner[a : a + 1, :] == owners, 1.0, 0.0) for a in range(8)]


def place_onehots(member):
    before = lax.broadcasted_iota(jnp.int32, (LANES, LANES), 0)
    after = lax.broadcasted_iota(jnp.int32, (LANES, LANES), 1)
    prefix = jnp.where(before < after, 1.0, 0.0).astype(jnp.bfloat16)
    above = [jnp.zeros((LANES, LANES), jnp.float32)]
    for m in member:
        above.append(above[-1] + m)
    left_of = jnp.dot(above[8].astype(jnp.bfloat16), prefix, preferred_element_type=jnp.float32)
    places = lax.broadcasted_iota(jnp.int32, (CAP, LANES), 0).astype(jnp.float32)
    onehots = []
    for a in range(8):
        place = jnp.sum(member[a] * (left_of + above[a]), axis=0, keepdims=True)
        onehots.append(jnp.where(places == place, 1.0, 0.0))
    return onehots


def placed(member, onehots, values):
    left = []
    for a in range(8):
        pieces = [onehots[a] * v[a : a + 1, :] for v in values]
        left.append(jnp.concatenate(pieces, axis=0).astype(jnp.bfloat16))
    return lax.dot_general(
        jnp.concatenate(left, axis=1),
        jnp.concatenate([m.astype(jnp.bfloat16) for m in member], axis=1),
        (((1,), (1,)), ((), ())),
        preferred_element_type=jnp.float32,
    )


def plan_kernel(ids_ref, request_ref, lanes_ref, places_ref):
    ids = as_lanes(ids_ref)
    lanes_ref[...] = ids
    row = ids & 2047
    high = (row >> 4).astype(jnp.float32)
    low = (row & 15).astype(jnp.float32)
    member = members(ids >> 11)
    onehots = place_onehots(member)
    for a in range(8):
        places_ref[a * CAP : (a + 1) * CAP, :] = onehots[a]
    table = placed(member, onehots, [high, low])
    wanted = (table[:CAP, :] * 16.0 + table[CAP:, :]).astype(jnp.int32)
    padded = jnp.concatenate([wanted, jnp.zeros((LANES - CAP, LANES), jnp.int32)], axis=0)
    request_ref[...] = padded.T


def slot_stages(ids_ref, places_ref, reader_ref, info_ref, reader_scratch):
    reader_scratch[...] = log_normalize(reader_ref[...])
    yield
    log_reader = as_lanes(reader_scratch)
    number = 4 * lax.broadcasted_iota(jnp.int32, (8, LANES), 0) + (
        lax.broadcasted_iota(jnp.int32, (8, LANES), 1) >> 5
    )
    part0 = log_reader.astype(jnp.bfloat16).astype(jnp.float32)
    rest = log_reader - part0
    part1 = rest.astype(jnp.bfloat16).astype(jnp.float32)
    part2 = rest - part1
    yield
    member = members(ids_ref[...] >> 11)
    yield
    values = [(number + 1).astype(jnp.float32), part0, part1, part2]
    onehots = [places_ref[a * CAP : (a + 1) * CAP, :] for a in range(8)]
    table = placed(member, onehots, values)
    yield
    group = LANES // 4
    wide_count = group * CAP
    owners = lax.broadcasted_iota(jnp.int32, (group, wide_count), 0)
    lanes = lax.broadcasted_iota(jnp.int32, (group, wide_count), 1)
    spread = jnp.where((lanes >> 4) == owners, 1.0, 0.0).astype(jnp.bfloat16)
    own = (lanes[:CAP] & (CAP - 1)) == owners[:CAP]
    for n in range(4):
        start = n * wide_count
        part = table[:, n * group : (n + 1) * group].astype(jnp.bfloat16)
        wide = jnp.dot(part, spread, preferred_element_type=jnp.float32)
        yield
        picked = [
            jnp.sum(jnp.where(own, wide[m * CAP : (m + 1) * CAP, :], 0.0), axis=0, keepdims=True)
            for m in range(4)
        ]
        question = picked[0] - 1.0
        log_part = picked[1] + picked[2] + picked[3]
        reader = jnp.where(question >= 0.0, jnp.exp(log_part), 0.0)
        fill = jnp.zeros((5, wide_count), jnp.float32)
        info_ref[:, start : start + wide_count] = jnp.concatenate(
            [question, log_part, reader, fill], axis=0
        )
        yield


def fetch_kernel(
    wanted_ref,
    passages_ref,
    ids_ref,
    places_ref,
    reader_ref,
    rows_ref,
    info_ref,
    image,
    even,
    odd,
    dense,
    reader_scratch,
    index,
    sem,
):
    count, width = passages_ref.shape
    chunks = width // LANES
    total = jnp.zeros((CAP, LANES), jnp.int32)
    for k in range(8):
        part = wanted_ref[pl.ds(k, 16, stride=8), :]
        total = total + (pltpu.roll(part, CAP * k, 1) if k else part)
    dense[...] = total
    copy = pltpu.make_async_copy(dense, index, sem)
    copy.start()
    for c in range(chunks):
        image[c * STRIDE : c * STRIDE + count, :] = passages_ref[
            :, c * LANES : (c + 1) * LANES
        ].astype(jnp.float32)
    stages = slot_stages(ids_ref, places_ref, reader_ref, info_ref, reader_scratch)
    next(stages)
    copy.wait()

    def move(line, moved):
        for k in range(LANES):
            r = index[line, k]
            moved[pl.ds(k, chunks, stride=STEP), :] = image[pl.ds(r, chunks, stride=STRIDE), :]

    def pack(line, moved):
        for c in range(chunks):
            rows_ref[line * LANES : (line + 1) * LANES, c * LANES : (c + 1) * LANES] = moved[
                c * STEP : c * STEP + LANES, :
            ].astype(rows_ref.dtype)

    buffers = (even, odd)
    move(0, even)
    for line in range(1, CAP):
        move(line, buffers[line % 2])
        next(stages, None)
        pack(line - 1, buffers[(line - 1) % 2])
    for _ in stages:
        pass
    pack(CAP - 1, odd)


def inner(left, right):
    return lax.dot_general(
        left, right, (((1,), (1,)), ((), ())), preferred_element_type=jnp.float32
    )


def score_kernel(questions_ref, rows_ref, info_ref, weights_ref, part_ref):
    count, width = questions_ref.shape
    scale = 4.0 / math.sqrt(width)
    questions = questions_ref[...]
    block = rows_ref.shape[0] // 8
    pieces = []
    for n in range(8):
        rows = rows_ref[n * block : (n + 1) * block, :]
        pieces.append(inner(rows, questions).T if n % 2 else inner(questions, rows))
    scores = jnp.concatenate(pieces, axis=1) * scale
    log_reader = info_ref[1:2, :]
    reader = info_ref[2:3, :]
    mine = info_ref[0:1, :] == lax.broadcasted_iota(jnp.int32, scores.shape, 0).astype(jnp.float32)
    masked = jnp.where(mine, scores, -jnp.inf)
    shifted = masked - jnp.max(masked, axis=1, keepdims=True)
    own = jnp.sum(jnp.where(mine, shifted, 0.0), axis=0, keepdims=True)
    known = jnp.sum(reader * (log_reader - own), axis=1, keepdims=True)
    mass = jnp.sum(jnp.where(mine, reader, 0.0), axis=1, keepdims=True)
    log_total = jnp.log(jnp.sum(jnp.exp(shifted), axis=1, keepdims=True))
    gap = jnp.exp(shifted - log_total) - reader
    weights_ref[...] = jnp.where(mine, gap, 0.0).astype(jnp.bfloat16)
    divergence = known + jnp.sum(mass * log_total, axis=0, keepdims=True)
    total = divergence / (count * part_ref.shape[0])
    part_ref[...] = jnp.broadcast_to(total, part_ref.shape)


def finish_kernel(sums_ref, weights_ref, rows_ref, mean_ref, grads_ref):
    scale = 4.0 / math.sqrt(rows_ref.shape[1])
    mean_ref[...] = jnp.sum(sums_ref[...], axis=0, keepdims=True)[:, :1]
    grads_ref[...] = (
        jnp.dot(weights_ref[...], rows_ref[...], preferred_element_type=jnp.float32) * scale
    )


def body(questions, passages, candidate_ids, reader_loglik):
    owners = lax.axis_size(AXES)
    question_count, width = questions.shape
    slot_count = owners * CAP
    request, lanes, places = pl.pallas_call(
        plan_kernel,
        out_shape=(
            pltpu.VMEM((owners, LANES), jnp.int32),
            pltpu.VMEM((8, LANES), jnp.int32),
            pltpu.VMEM((8 * CAP, LANES), jnp.float32),
        ),
        in_specs=[VMEM],
        out_specs=(VMEM, VMEM, VMEM),
        cost_estimate=pl.CostEstimate(flops=1 << 30, transcendentals=0, bytes_accessed=0),
        compiler_params=PARAMS,
        name="plan",
    )(candidate_ids)
    wanted = exchange(request)
    fetched, info = pl.pallas_call(
        fetch_kernel,
        out_shape=(
            pltpu.VMEM((slot_count, width), passages.dtype),
            pltpu.VMEM((8, slot_count), jnp.float32),
        ),
        in_specs=[VMEM, VMEM, VMEM, VMEM, VMEM],
        out_specs=(VMEM, VMEM),
        scratch_shapes=[
            pltpu.VMEM((width // LANES * STRIDE, LANES), jnp.float32),
            pltpu.VMEM((width // LANES * STEP, LANES), jnp.float32),
            pltpu.VMEM((width // LANES * STEP, LANES), jnp.float32),
            pltpu.VMEM((CAP, LANES), jnp.int32),
            pltpu.VMEM(reader_loglik.shape, jnp.float32),
            pltpu.SMEM((CAP, LANES), jnp.int32),
            pltpu.SemaphoreType.DMA,
        ],
        compiler_params=PARAMS,
        name="fetch",
    )(wanted, in_vmem(passages), in_vmem(lanes), in_vmem(places), in_vmem(reader_loglik))
    replies = exchange(fetched.reshape(owners, CAP, width)).reshape(slot_count, width)
    replies = in_vmem(replies)
    weights, part = pl.pallas_call(
        score_kernel,
        out_shape=(
            pltpu.VMEM((question_count, slot_count), jnp.bfloat16),
            pltpu.VMEM((owners, LANES), jnp.float32),
        ),
        in_specs=[VMEM, VMEM, VMEM],
        out_specs=(VMEM, VMEM),
        compiler_params=PARAMS,
        name="score",
    )(questions, replies, info)
    mean, grads = pl.pallas_call(
        finish_kernel,
        out_shape=(
            jax.ShapeDtypeStruct((1, 1), jnp.float32),
            jax.ShapeDtypeStruct((question_count, width), jnp.float32),
        ),
        in_specs=[VMEM, VMEM, VMEM],
        out_specs=(VMEM, VMEM),
        compiler_params=PARAMS,
        name="finish",
    )(exchange(part), weights, replies)
    return (mean.reshape(()), grads)


def solution(mesh):
    placed = P(AXES, None)
    return jax.shard_map(
        body,
        mesh=mesh,
        in_specs=(placed, placed, placed, placed),
        out_specs=(P(), placed),
        check_vma=False,
    )
```

```python
import math

import jax
import jax.numpy as jnp
from jax import lax
from jax.experimental import pallas as pl
from jax.experimental.pallas import tpu as pltpu
from jax.sharding import PartitionSpec as P

AXES = ("index", "bulk")
LANES = 128
CAP = 16
STRIDE = 2048 + 4
STEP = LANES + 4
VMEM = pl.BlockSpec(memory_space=pltpu.VMEM)
HBM = pl.BlockSpec(memory_space=pltpu.HBM)
PARAMS = pltpu.CompilerParams(vmem_limit_bytes=24 << 20)


def in_vmem(array):
    return pltpu.with_memory_space_constraint(array, pltpu.VMEM)


def in_hbm(array):
    return pltpu.with_memory_space_constraint(array, pltpu.HBM)


def exchange(blocks):
    return lax.all_to_all(blocks, AXES, split_axis=0, concat_axis=0, tiled=True)


def log_normalize(logits):
    highest = jnp.max(logits, axis=1, keepdims=True)
    shifted = logits - highest
    return shifted - jnp.log(jnp.sum(jnp.exp(shifted), axis=1, keepdims=True))


def as_lanes(ref):
    return jnp.concatenate([ref[pl.ds(b, 8, stride=4), :] for b in range(4)], axis=1)


def members(owner):
    owners = lax.broadcasted_iota(jnp.int32, (LANES, LANES), 0)
    return [jnp.where(owner[a : a + 1, :] == owners, 1.0, 0.0) for a in range(8)]


def place_onehots(member):
    before = lax.broadcasted_iota(jnp.int32, (LANES, LANES), 0)
    after = lax.broadcasted_iota(jnp.int32, (LANES, LANES), 1)
    prefix = jnp.where(before < after, 1.0, 0.0).astype(jnp.bfloat16)
    above = [jnp.zeros((LANES, LANES), jnp.float32)]
    for m in member:
        above.append(above[-1] + m)
    left_of = jnp.dot(above[8].astype(jnp.bfloat16), prefix, preferred_element_type=jnp.float32)
    places = lax.broadcasted_iota(jnp.int32, (CAP, LANES), 0).astype(jnp.float32)
    onehots = []
    for a in range(8):
        place = jnp.sum(member[a] * (left_of + above[a]), axis=0, keepdims=True)
        onehots.append(jnp.where(places == place, 1.0, 0.0))
    return onehots


def placed(member, onehots, values):
    left = []
    for a in range(8):
        pieces = [onehots[a] * v[a : a + 1, :] for v in values]
        left.append(jnp.concatenate(pieces, axis=0).astype(jnp.bfloat16))
    return lax.dot_general(
        jnp.concatenate(left, axis=1),
        jnp.concatenate([m.astype(jnp.bfloat16) for m in member], axis=1),
        (((1,), (1,)), ((), ())),
        preferred_element_type=jnp.float32,
    )


def plan_kernel(ids_ref, request_ref, lanes_ref, places_ref):
    ids = as_lanes(ids_ref)
    lanes_ref[...] = ids
    row = ids & 2047
    high = (row >> 4).astype(jnp.float32)
    low = (row & 15).astype(jnp.float32)
    member = members(ids >> 11)
    onehots = place_onehots(member)
    for a in range(8):
        places_ref[a * CAP : (a + 1) * CAP, :] = onehots[a]
    table = placed(member, onehots, [high, low])
    wanted = (table[:CAP, :] * 16.0 + table[CAP:, :]).astype(jnp.int32)
    padded = jnp.concatenate([wanted, jnp.zeros((LANES - CAP, LANES), jnp.int32)], axis=0)
    request_ref[...] = padded.T


def slot_stages(ids_ref, places_ref, reader_ref, info_ref, reader_scratch):
    reader_scratch[...] = log_normalize(reader_ref[...])
    yield
    log_reader = as_lanes(reader_scratch)
    number = 4 * lax.broadcasted_iota(jnp.int32, (8, LANES), 0) + (
        lax.broadcasted_iota(jnp.int32, (8, LANES), 1) >> 5
    )
    part0 = log_reader.astype(jnp.bfloat16).astype(jnp.float32)
    rest = log_reader - part0
    part1 = rest.astype(jnp.bfloat16).astype(jnp.float32)
    part2 = rest - part1
    yield
    member = members(ids_ref[...] >> 11)
    yield
    values = [(number + 1).astype(jnp.float32), part0, part1, part2]
    onehots = [places_ref[a * CAP : (a + 1) * CAP, :] for a in range(8)]
    table = placed(member, onehots, values)
    yield
    group = LANES // 4
    wide_count = group * CAP
    owners = lax.broadcasted_iota(jnp.int32, (group, wide_count), 0)
    lanes = lax.broadcasted_iota(jnp.int32, (group, wide_count), 1)
    spread = jnp.where((lanes >> 4) == owners, 1.0, 0.0).astype(jnp.bfloat16)
    own = (lanes[:CAP] & (CAP - 1)) == owners[:CAP]
    for n in range(4):
        start = n * wide_count
        part = table[:, n * group : (n + 1) * group].astype(jnp.bfloat16)
        wide = jnp.dot(part, spread, preferred_element_type=jnp.float32)
        yield
        picked = [
            jnp.sum(jnp.where(own, wide[m * CAP : (m + 1) * CAP, :], 0.0), axis=0, keepdims=True)
            for m in range(4)
        ]
        question = picked[0] - 1.0
        log_part = picked[1] + picked[2] + picked[3]
        reader = jnp.where(question >= 0.0, jnp.exp(log_part), 0.0)
        fill = jnp.zeros((5, wide_count), jnp.float32)
        info_ref[:, start : start + wide_count] = jnp.concatenate(
            [question, log_part, reader, fill], axis=0
        )
        yield


def fetch_kernel(
    wanted_ref,
    passages_ref,
    ids_ref,
    places_ref,
    reader_ref,
    rows_ref,
    info_ref,
    image,
    even,
    odd,
    dense,
    reader_scratch,
    index,
    sem,
):
    count, width = passages_ref.shape
    chunks = width // LANES
    total = jnp.zeros((CAP, LANES), jnp.int32)
    for k in range(8):
        part = wanted_ref[pl.ds(k, 16, stride=8), :]
        total = total + (pltpu.roll(part, CAP * k, 1) if k else part)
    dense[...] = total
    copy = pltpu.make_async_copy(dense, index, sem)
    copy.start()
    for c in range(chunks):
        image[c * STRIDE : c * STRIDE + count, :] = passages_ref[
            :, c * LANES : (c + 1) * LANES
        ].astype(jnp.float32)
    stages = slot_stages(ids_ref, places_ref, reader_ref, info_ref, reader_scratch)
    next(stages)
    copy.wait()

    def move(line, moved):
        for k in range(LANES):
            r = index[line, k]
            moved[pl.ds(k, chunks, stride=STEP), :] = image[pl.ds(r, chunks, stride=STRIDE), :]

    def pack(line, moved):
        for g in range(0, LANES, 16):
            block = [moved[c * STEP + g : c * STEP + g + 16, :] for c in range(chunks)]
            rows_ref[line * LANES + g : line * LANES + g + 16, :] = jnp.concatenate(
                block, axis=1
            ).astype(rows_ref.dtype)

    buffers = (even, odd)
    move(0, even)
    for line in range(1, CAP):
        move(line, buffers[line % 2])
        next(stages, None)
        pack(line - 1, buffers[(line - 1) % 2])
    for _ in stages:
        pass
    pack(CAP - 1, odd)


def inner(left, right):
    return lax.dot_general(
        left, right, (((1,), (1,)), ((), ())), preferred_element_type=jnp.float32
    )


def score_kernel(questions_ref, rows_ref, info_ref, weights_ref, part_ref):
    count, width = questions_ref.shape
    scale = 4.0 / math.sqrt(width)
    questions = questions_ref[...]
    block = rows_ref.shape[0] // 8
    pieces = []
    for n in range(8):
        rows = rows_ref[n * block : (n + 1) * block, :]
        pieces.append(inner(rows, questions).T if n % 2 else inner(questions, rows))
    scores = jnp.concatenate(pieces, axis=1) * scale
    log_reader = info_ref[1:2, :]
    reader = info_ref[2:3, :]
    mine = info_ref[0:1, :] == lax.broadcasted_iota(jnp.int32, scores.shape, 0).astype(jnp.float32)
    masked = jnp.where(mine, scores, -jnp.inf)
    shifted = masked - jnp.max(masked, axis=1, keepdims=True)
    own = jnp.sum(jnp.where(mine, shifted, 0.0), axis=0, keepdims=True)
    known = jnp.sum(reader * (log_reader - own), axis=1, keepdims=True)
    mass = jnp.sum(jnp.where(mine, reader, 0.0), axis=1, keepdims=True)
    log_total = jnp.log(jnp.sum(jnp.exp(shifted), axis=1, keepdims=True))
    gap = jnp.exp(shifted - log_total) - reader
    weights_ref[...] = jnp.where(mine, gap, 0.0).astype(jnp.bfloat16)
    divergence = known + jnp.sum(mass * log_total, axis=0, keepdims=True)
    total = divergence / (count * part_ref.shape[0])
    part_ref[...] = jnp.broadcast_to(total, part_ref.shape)


def finish_kernel(sums_ref, weights_ref, rows_ref, mean_ref, grads_ref):
    scale = 4.0 / math.sqrt(rows_ref.shape[1])
    mean_ref[...] = jnp.sum(sums_ref[...], axis=0, keepdims=True)[:, :1]
    grads_ref[...] = (
        jnp.dot(weights_ref[...], rows_ref[...], preferred_element_type=jnp.float32) * scale
    )


def body(questions, passages, candidate_ids, reader_loglik):
    owners = lax.axis_size(AXES)
    question_count, width = questions.shape
    slot_count = owners * CAP
    request, lanes, places = pl.pallas_call(
        plan_kernel,
        out_shape=(
            pltpu.VMEM((owners, LANES), jnp.int32),
            pltpu.VMEM((8, LANES), jnp.int32),
            pltpu.VMEM((8 * CAP, LANES), jnp.float32),
        ),
        in_specs=[VMEM],
        out_specs=(VMEM, VMEM, VMEM),
        cost_estimate=pl.CostEstimate(flops=1 << 30, transcendentals=0, bytes_accessed=0),
        compiler_params=PARAMS,
        name="plan",
    )(candidate_ids)
    wanted = exchange(request)
    fetched, info = pl.pallas_call(
        fetch_kernel,
        out_shape=(
            pltpu.VMEM((slot_count, width), passages.dtype),
            pltpu.VMEM((8, slot_count), jnp.float32),
        ),
        in_specs=[VMEM, VMEM, VMEM, VMEM, VMEM],
        out_specs=(VMEM, VMEM),
        scratch_shapes=[
            pltpu.VMEM((width // LANES * STRIDE, LANES), jnp.float32),
            pltpu.VMEM((width // LANES * STEP, LANES), jnp.float32),
            pltpu.VMEM((width // LANES * STEP, LANES), jnp.float32),
            pltpu.VMEM((CAP, LANES), jnp.int32),
            pltpu.VMEM(reader_loglik.shape, jnp.float32),
            pltpu.SMEM((CAP, LANES), jnp.int32),
            pltpu.SemaphoreType.DMA,
        ],
        compiler_params=PARAMS,
        name="fetch",
    )(wanted, in_vmem(passages), in_vmem(lanes), in_vmem(places), in_vmem(reader_loglik))
    replies = exchange(fetched.reshape(owners, CAP, width)).reshape(slot_count, width)
    replies = in_vmem(replies)
    weights, part = pl.pallas_call(
        score_kernel,
        out_shape=(
            pltpu.VMEM((question_count, slot_count), jnp.bfloat16),
            pltpu.VMEM((owners, LANES), jnp.float32),
        ),
        in_specs=[VMEM, VMEM, VMEM],
        out_specs=(VMEM, VMEM),
        compiler_params=PARAMS,
        name="score",
    )(questions, replies, info)
    mean, grads = pl.pallas_call(
        finish_kernel,
        out_shape=(
            jax.ShapeDtypeStruct((1, 1), jnp.float32),
            jax.ShapeDtypeStruct((question_count, width), jnp.float32),
        ),
        in_specs=[VMEM, VMEM, VMEM],
        out_specs=(VMEM, VMEM),
        compiler_params=PARAMS,
        name="finish",
    )(exchange(part), weights, replies)
    return (mean.reshape(()), grads)


def solution(mesh):
    placed = P(AXES, None)
    return jax.shard_map(
        body,
        mesh=mesh,
        in_specs=(placed, placed, placed, placed),
        out_specs=(P(), placed),
        check_vma=False,
    )
```

```python
import math

import jax
import jax.numpy as jnp
from jax import lax
from jax.experimental import pallas as pl
from jax.experimental.pallas import tpu as pltpu
from jax.sharding import PartitionSpec as P

AXES = ("index", "bulk")
LANES = 128
CAP = 16
STRIDE = 2048 + 4
STEP = LANES + 4
VMEM = pl.BlockSpec(memory_space=pltpu.VMEM)
HBM = pl.BlockSpec(memory_space=pltpu.HBM)
PARAMS = pltpu.CompilerParams(vmem_limit_bytes=24 << 20)


def in_vmem(array):
    return pltpu.with_memory_space_constraint(array, pltpu.VMEM)


def in_hbm(array):
    return pltpu.with_memory_space_constraint(array, pltpu.HBM)


def exchange(blocks):
    return lax.all_to_all(blocks, AXES, split_axis=0, concat_axis=0, tiled=True)


def log_normalize(logits):
    highest = jnp.max(logits, axis=1, keepdims=True)
    shifted = logits - highest
    return shifted - jnp.log(jnp.sum(jnp.exp(shifted), axis=1, keepdims=True))


def as_lanes(ref):
    return jnp.concatenate([ref[pl.ds(b, 8, stride=4), :] for b in range(4)], axis=1)


def members(owner):
    owners = lax.broadcasted_iota(jnp.int32, (LANES, LANES), 0)
    return [jnp.where(owner[a : a + 1, :] == owners, 1.0, 0.0) for a in range(8)]


def place_onehots(member):
    before = lax.broadcasted_iota(jnp.int32, (LANES, LANES), 0)
    after = lax.broadcasted_iota(jnp.int32, (LANES, LANES), 1)
    prefix = jnp.where(before < after, 1.0, 0.0).astype(jnp.bfloat16)
    above = [jnp.zeros((LANES, LANES), jnp.float32)]
    for m in member:
        above.append(above[-1] + m)
    left_of = jnp.dot(above[8].astype(jnp.bfloat16), prefix, preferred_element_type=jnp.float32)
    places = lax.broadcasted_iota(jnp.int32, (CAP, LANES), 0).astype(jnp.float32)
    onehots = []
    for a in range(8):
        place = jnp.sum(member[a] * (left_of + above[a]), axis=0, keepdims=True)
        onehots.append(jnp.where(places == place, 1.0, 0.0))
    return onehots


def placed(member, onehots, values):
    left = []
    for a in range(8):
        pieces = [onehots[a] * v[a : a + 1, :] for v in values]
        left.append(jnp.concatenate(pieces, axis=0).astype(jnp.bfloat16))
    return lax.dot_general(
        jnp.concatenate(left, axis=1),
        jnp.concatenate([m.astype(jnp.bfloat16) for m in member], axis=1),
        (((1,), (1,)), ((), ())),
        preferred_element_type=jnp.float32,
    )


def plan_kernel(ids_ref, request_ref, lanes_ref, places_ref):
    ids = as_lanes(ids_ref)
    lanes_ref[...] = ids
    row = ids & 2047
    high = (row >> 4).astype(jnp.float32)
    low = (row & 15).astype(jnp.float32)
    member = members(ids >> 11)
    onehots = place_onehots(member)
    for a in range(8):
        places_ref[a * CAP : (a + 1) * CAP, :] = onehots[a]
    table = placed(member, onehots, [high, low])
    wanted = (table[:CAP, :] * 16.0 + table[CAP:, :]).astype(jnp.int32)
    padded = jnp.concatenate([wanted, jnp.zeros((LANES - CAP, LANES), jnp.int32)], axis=0)
    request_ref[...] = padded.T


def slot_stages(ids_ref, places_ref, reader_ref, info_ref, reader_scratch):
    reader_scratch[...] = log_normalize(reader_ref[...])
    yield
    log_reader = as_lanes(reader_scratch)
    number = 4 * lax.broadcasted_iota(jnp.int32, (8, LANES), 0) + (
        lax.broadcasted_iota(jnp.int32, (8, LANES), 1) >> 5
    )
    part0 = log_reader.astype(jnp.bfloat16).astype(jnp.float32)
    rest = log_reader - part0
    part1 = rest.astype(jnp.bfloat16).astype(jnp.float32)
    part2 = rest - part1
    yield
    member = members(ids_ref[...] >> 11)
    yield
    values = [(number + 1).astype(jnp.float32), part0, part1, part2]
    onehots = [places_ref[a * CAP : (a + 1) * CAP, :] for a in range(8)]
    table = placed(member, onehots, values)
    yield
    group = LANES // 4
    wide_count = group * CAP
    owners = lax.broadcasted_iota(jnp.int32, (group, wide_count), 0)
    lanes = lax.broadcasted_iota(jnp.int32, (group, wide_count), 1)
    spread = jnp.where((lanes >> 4) == owners, 1.0, 0.0).astype(jnp.bfloat16)
    own = (lanes[:CAP] & (CAP - 1)) == owners[:CAP]
    for n in range(4):
        start = n * wide_count
        part = table[:, n * group : (n + 1) * group].astype(jnp.bfloat16)
        wide = jnp.dot(part, spread, preferred_element_type=jnp.float32)
        yield
        picked = [
            jnp.sum(jnp.where(own, wide[m * CAP : (m + 1) * CAP, :], 0.0), axis=0, keepdims=True)
            for m in range(4)
        ]
        question = picked[0] - 1.0
        log_part = picked[1] + picked[2] + picked[3]
        reader = jnp.where(question >= 0.0, jnp.exp(log_part), 0.0)
        fill = jnp.zeros((5, wide_count), jnp.float32)
        info_ref[:, start : start + wide_count] = jnp.concatenate(
            [question, log_part, reader, fill], axis=0
        )
        yield


def fetch_kernel(
    wanted_ref,
    passages_ref,
    ids_ref,
    places_ref,
    reader_ref,
    rows_ref,
    info_ref,
    image,
    even,
    odd,
    dense,
    reader_scratch,
    index,
    sem,
):
    count, width = passages_ref.shape
    chunks = width // LANES
    total = jnp.zeros((CAP, LANES), jnp.int32)
    for k in range(8):
        part = wanted_ref[pl.ds(k, 16, stride=8), :]
        total = total + (pltpu.roll(part, CAP * k, 1) if k else part)
    dense[...] = total
    copy = pltpu.make_async_copy(dense, index, sem)
    copy.start()
    for c in range(chunks):
        image[c * STRIDE : c * STRIDE + count, :] = passages_ref[
            :, c * LANES : (c + 1) * LANES
        ].astype(jnp.float32)
    stages = slot_stages(ids_ref, places_ref, reader_ref, info_ref, reader_scratch)
    next(stages)
    copy.wait()

    def move(line, moved):
        for k in range(LANES):
            r = index[line, k]
            moved[pl.ds(k, chunks, stride=STEP), :] = image[pl.ds(r, chunks, stride=STRIDE), :]

    def pack(line, moved):
        for g in range(0, LANES, 16):
            block = [moved[c * STEP + g : c * STEP + g + 16, :] for c in range(chunks)]
            rows_ref[line * LANES + g : line * LANES + g + 16, :] = jnp.concatenate(
                block, axis=1
            ).astype(rows_ref.dtype)

    buffers = (even, odd)
    move(0, even)
    for line in range(1, CAP):
        move(line, buffers[line % 2])
        next(stages, None)
        pack(line - 1, buffers[(line - 1) % 2])
    for _ in stages:
        pass
    pack(CAP - 1, odd)


def inner(left, right):
    return lax.dot_general(
        left, right, (((1,), (1,)), ((), ())), preferred_element_type=jnp.float32
    )


def score_kernel(questions_ref, rows_ref, info_ref, weights_ref, part_ref):
    count, width = questions_ref.shape
    scale = 4.0 / math.sqrt(width)
    questions = questions_ref[...]
    block = rows_ref.shape[0] // 8
    pieces = []
    for n in range(8):
        rows = rows_ref[n * block : (n + 1) * block, :]
        pieces.append(inner(questions, rows) if n % 2 else inner(rows, questions).T)
    scores = jnp.concatenate(pieces, axis=1) * scale
    log_reader = info_ref[1:2, :]
    reader = info_ref[2:3, :]
    mine = info_ref[0:1, :] == lax.broadcasted_iota(jnp.int32, scores.shape, 0).astype(jnp.float32)
    masked = jnp.where(mine, scores, -jnp.inf)
    shifted = masked - jnp.max(masked, axis=1, keepdims=True)
    own = jnp.sum(jnp.where(mine, shifted, 0.0), axis=0, keepdims=True)
    known = jnp.sum(reader * (log_reader - own), axis=1, keepdims=True)
    mass = jnp.sum(jnp.where(mine, reader, 0.0), axis=1, keepdims=True)
    log_total = jnp.log(jnp.sum(jnp.exp(shifted), axis=1, keepdims=True))
    gap = jnp.exp(shifted - log_total) - reader
    weights_ref[...] = jnp.where(mine, gap, 0.0).astype(jnp.bfloat16)
    divergence = known + jnp.sum(mass * log_total, axis=0, keepdims=True)
    total = divergence / (count * part_ref.shape[0])
    part_ref[...] = jnp.broadcast_to(total, part_ref.shape)


def finish_kernel(sums_ref, weights_ref, rows_ref, mean_ref, grads_ref):
    scale = 4.0 / math.sqrt(rows_ref.shape[1])
    mean_ref[...] = jnp.sum(sums_ref[...], axis=0, keepdims=True)[:, :1]
    grads_ref[...] = (
        jnp.dot(weights_ref[...], rows_ref[...], preferred_element_type=jnp.float32) * scale
    )


def body(questions, passages, candidate_ids, reader_loglik):
    owners = lax.axis_size(AXES)
    question_count, width = questions.shape
    slot_count = owners * CAP
    request, lanes, places = pl.pallas_call(
        plan_kernel,
        out_shape=(
            pltpu.VMEM((owners, LANES), jnp.int32),
            pltpu.VMEM((8, LANES), jnp.int32),
            pltpu.VMEM((8 * CAP, LANES), jnp.float32),
        ),
        in_specs=[VMEM],
        out_specs=(VMEM, VMEM, VMEM),
        cost_estimate=pl.CostEstimate(flops=1 << 30, transcendentals=0, bytes_accessed=0),
        compiler_params=PARAMS,
        name="plan",
    )(candidate_ids)
    wanted = exchange(request)
    fetched, info = pl.pallas_call(
        fetch_kernel,
        out_shape=(
            pltpu.VMEM((slot_count, width), passages.dtype),
            pltpu.VMEM((8, slot_count), jnp.float32),
        ),
        in_specs=[VMEM, VMEM, VMEM, VMEM, VMEM],
        out_specs=(VMEM, VMEM),
        scratch_shapes=[
            pltpu.VMEM((width // LANES * STRIDE, LANES), jnp.float32),
            pltpu.VMEM((width // LANES * STEP, LANES), jnp.float32),
            pltpu.VMEM((width // LANES * STEP, LANES), jnp.float32),
            pltpu.VMEM((CAP, LANES), jnp.int32),
            pltpu.VMEM(reader_loglik.shape, jnp.float32),
            pltpu.SMEM((CAP, LANES), jnp.int32),
            pltpu.SemaphoreType.DMA,
        ],
        compiler_params=PARAMS,
        name="fetch",
    )(wanted, in_vmem(passages), in_vmem(lanes), in_vmem(places), in_vmem(reader_loglik))
    replies = exchange(fetched.reshape(owners, CAP, width)).reshape(slot_count, width)
    replies = in_vmem(replies)
    weights, part = pl.pallas_call(
        score_kernel,
        out_shape=(
            pltpu.VMEM((question_count, slot_count), jnp.bfloat16),
            pltpu.VMEM((owners, LANES), jnp.float32),
        ),
        in_specs=[VMEM, VMEM, VMEM],
        out_specs=(VMEM, VMEM),
        compiler_params=PARAMS,
        name="score",
    )(questions, replies, info)
    mean, grads = pl.pallas_call(
        finish_kernel,
        out_shape=(
            jax.ShapeDtypeStruct((1, 1), jnp.float32),
            jax.ShapeDtypeStruct((question_count, width), jnp.float32),
        ),
        in_specs=[VMEM, VMEM, VMEM],
        out_specs=(VMEM, VMEM),
        compiler_params=PARAMS,
        name="finish",
    )(exchange(part), weights, replies)
    return (mean.reshape(()), grads)


def solution(mesh):
    placed = P(AXES, None)
    return jax.shard_map(
        body,
        mesh=mesh,
        in_specs=(placed, placed, placed, placed),
        out_specs=(P(), placed),
        check_vma=False,
    )
```
